256 devices in a mesh: feat: 8 (over y, core), clus: 32 (over z, x).
Axes of the slice: x: 4, y: 4, z: 8, core: 2. Of those that a mesh axis runs over, the one named last changes fastest.
Arguments:
- item_feats: bfloat16 [16384, 512], P('clus', 'feat'), may hold values from -6 to 6
- w_hidden: bfloat16 [512, 1024], P(None, 'feat'), may hold values from -0.25 to 0.25
- b_hidden: bfloat16 [1024], P('feat'), may hold values from -3 to 3
- w_out: bfloat16 [1024, 256], P('feat'), may hold values from -0.1875 to 0.1875
- item_cluster: int32 [16384], P('clus'), may hold values from 0 to 127, as said below
- cluster_slot: int32 [128], replicated, may hold values from 0 to 127, as said below
- catalog: bfloat16 [128, 256, 256], P('clus', 'feat'), may hold values from -0.375 to 0.375
- cluster_fill: int32 [128], P('clus'), may hold values from 32 to 256, as said below
- queries: bfloat16 [1024, 256], P('clus'), may hold values from -6 to 6
- probes: int32 [1024, 8], P('clus'), may hold values from 0 to 127, all different within a row
Outputs:
- best_scores: float32 [1024, 128], P('clus')
The draws below stay inside these ranges and needn't reach their ends.
Inputs may be any that keep to these rules, and one draw needn't show every extreme that they name: `item_cluster`: in every aligned block of 64 items (the rows of one device after the tower), at most 4 items lie in clusters of one owner, and this bound is reached in every block. `cluster_slot`: A permutation of the catalog positions. `cluster_fill`: rows of a cluster at and beyond its fill are padding. `probes`: the 8 ids of a query are distinct.
All inputs are finite; a program needn't handle non-finite values.
Results may differ from the reference program's by a relative error of at most 0.0011.
Values may be sent and summed in bfloat16 or wider, within the bound.
A program may use at most 256 MiB of HBM per device.

```python
import math
import jax
import jax.numpy as jnp
from jax import lax

EMB = 256
IN_W = 512
HID_W = 1024
ROWS_DEV = 64
CL_DEV = 4
ROW_DEV = 32
PROBES = 8
TOPK = 128
ITEMS = 16384
CLUSTERS = 128
CL_ROWS = 256
QUERIES = 1024


def slot_order(key):
    return jax.random.permutation(jax.random.fold_in(key, 3), CLUSTERS).astype(jnp.int32)


def draw_cluster_slot(key, part):
    return slot_order(key)


def shuffle_block(block_key):
    return jax.random.permutation(block_key, ROWS_DEV)


def draw_item_cluster(key, part):
    placing = slot_order(key)
    inverse = jnp.zeros((CLUSTERS,), jnp.int32).at[placing].set(jnp.arange(CLUSTERS, dtype=jnp.int32))
    owners = CLUSTERS // CL_DEV
    blocks = ITEMS // ROWS_DEV
    capacity = 2 * ROWS_DEV // owners
    first_hot = jax.random.randint(jax.random.fold_in(key, 5), (), 0, owners)
    offsets = jax.random.randint(jax.random.fold_in(key, 6), (blocks,), 0, owners - 1)
    second_hot = (first_hot + 1 + offsets) % owners
    rotation = jax.random.randint(jax.random.fold_in(key, 8), (blocks,), 0, owners - 2)
    row_index = jnp.arange(ROWS_DEV, dtype=jnp.int32)
    rest_index = jnp.maximum(row_index - 2 * capacity, 0)
    other_index = (rotation[:, None] + rest_index[None, :] % (owners - 2)) % (owners - 2)
    low_hot = jnp.minimum(first_hot, second_hot)[:, None]
    high_hot = jnp.maximum(first_hot, second_hot)[:, None]
    other_owner = other_index + (other_index >= low_hot).astype(jnp.int32)
    other_owner = other_owner + (other_owner >= high_hot).astype(jnp.int32)
    owner_label = jnp.where(row_index[None, :] < capacity, first_hot, jnp.where(row_index[None, :] < 2 * capacity, second_hot[:, None], other_owner))
    block_keys = jax.random.split(jax.random.fold_in(key, 9), blocks)
    row_order = jax.vmap(shuffle_block)(block_keys)
    owner_label = jnp.take_along_axis(owner_label, row_order, axis=1)
    local_part = jax.random.randint(jax.random.fold_in(key, 10), (blocks, ROWS_DEV), 0, CL_DEV)
    position = (owner_label * CL_DEV + local_part).reshape(ITEMS)
    return inverse[position].astype(jnp.int32)


def draw_cluster_fill(key, part):
    fill_rows = jax.random.randint(jax.random.fold_in(key, 12), (CLUSTERS,), ROW_DEV, CL_ROWS + 1)
    full_pick = jax.random.randint(jax.random.fold_in(key, 13), (), 0, CLUSTERS)
    step_pick = jax.random.randint(jax.random.fold_in(key, 14), (), 0, CLUSTERS - 1)
    least_pick = (full_pick + 1 + step_pick) % CLUSTERS
    fill_rows = fill_rows.at[full_pick].set(CL_ROWS)
    fill_rows = fill_rows.at[least_pick].set(ROW_DEV)
    return fill_rows.astype(jnp.int32)


def steps_of(own_key, shape, shards, least, high):
    def one(axis_at, parts):
        steps = jax.random.uniform(jax.random.fold_in(jax.random.fold_in(own_key, 6), axis_at), (parts,), jnp.float32, least / len(shards), high / len(shards))
        return jnp.repeat(jnp.exp(steps), shape[axis_at] // parts).reshape((-1,) + (1,) * (len(shape) - axis_at - 1))

    factor_of = one(*shards[0])
    for cut in shards[1:]:
        factor_of = factor_of * one(*cut)
    return factor_of


def different_ones(rng, rows, count, top, lift):
    sequence = jax.random.permutation(jax.random.fold_in(rng, 1), count)
    pull = sequence
    for power in range(3):
        pull = pull * pull // count
    pull = pull * lift // count
    chance = jax.random.randint(jax.random.fold_in(rng, 2), (rows, count), 0, 4096) + pull
    fixed_rows = jax.random.permutation(jax.random.fold_in(rng, 3), rows)[jnp.arange(count) % rows]
    chance = jnp.where(jnp.arange(rows)[:, None] == fixed_rows[None, :], 1 << 14, chance)
    score = chance * count + jnp.arange(count)
    return lax.top_k(score.astype(jnp.int32), top)[1].astype(jnp.int32)


def noise(own_key, dims, width, limit, pieces=(), held_as=jnp.bfloat16):
    drawn = jax.random.normal(own_key, dims, jnp.float32) * width
    if len(pieces) > 0:
        drawn = steps_of(own_key, dims, pieces, -0.22, 0.18) * drawn
    return jnp.clip(drawn, min=-limit, max=limit).astype(held_as)


def setup_inputs(seed: int = 0) -> dict:
    arg_keys = jax.random.split(jax.random.key(seed), 11)
    item_feats = noise(arg_keys[0], (ITEMS, IN_W), 1.0, 6.0, ((0, 32), (1, 8)))
    w_hidden = noise(arg_keys[1], (IN_W, HID_W), IN_W ** -0.5, 0.25, ((1, 8),))
    b_hidden = noise(arg_keys[2], (HID_W,), 0.5, 3.0, ((0, 8),))
    w_out = noise(arg_keys[3], (HID_W, EMB), HID_W ** -0.5, 0.1875, ((0, 8),))
    item_cluster = draw_item_cluster(jax.random.fold_in(arg_keys[10], 71), 0)
    cluster_slot = draw_cluster_slot(jax.random.fold_in(arg_keys[10], 71), 0)
    catalog = noise(arg_keys[6], (CLUSTERS, CL_ROWS, EMB), 0.0625, 0.375, ((0, 32), (1, 8)))
    cluster_fill = draw_cluster_fill(jax.random.fold_in(arg_keys[10], 71), 0)
    queries = noise(arg_keys[8], (QUERIES, EMB), 1.0, 6.0, ((0, 32),))
    probes = different_ones(arg_keys[9], QUERIES, CLUSTERS, PROBES, 512)
    return dict(item_feats=item_feats, w_hidden=w_hidden, b_hidden=b_hidden, w_out=w_out, item_cluster=item_cluster, cluster_slot=cluster_slot, catalog=catalog, cluster_fill=cluster_fill, queries=queries, probes=probes)


masked_score = -1e+30
unit_scale = 0.0625

def reference(item_feats, w_hidden, b_hidden, w_out, item_cluster, cluster_slot, catalog, cluster_fill, queries, probes):
    pre_act = jnp.dot(item_feats, w_hidden, preferred_element_type=jnp.float32) + b_hidden.astype(jnp.float32)
    hidden = jax.nn.silu(pre_act).astype(jnp.bfloat16)
    projected = jnp.dot(hidden, w_out, preferred_element_type=jnp.float32)
    scaling = lax.rsqrt(lax.optimization_barrier(jnp.mean(projected * projected, axis=1, keepdims=True)) + 1e-06) * unit_scale
    embedded = (projected * scaling).astype(jnp.bfloat16)
    item_places = cluster_slot[item_cluster]
    probe_places = cluster_slot[probes]
    stored_live = jnp.arange(CL_ROWS, dtype=jnp.int32)[None, :] < cluster_fill[:, None]
    stored = catalog.astype(jnp.float32).reshape(CLUSTERS * CL_ROWS, EMB)
    fresh = embedded.astype(jnp.float32)
    block_rows = math.gcd(QUERIES, 256)
    cluster_ids = jnp.arange(CLUSTERS, dtype=jnp.int32)
    per_cluster = min(TOPK, CL_ROWS)

    def score_block(inputs):
        query_rows, probe_rows = inputs
        query_f32 = query_rows.astype(jnp.float32)
        probed = jnp.any(probe_rows[:, :, None] == cluster_ids[None, None, :], axis=1)
        stored_scores = jnp.einsum('bd,rd->br', query_f32, stored, precision=lax.Precision.HIGHEST)
        stored_scores = stored_scores.reshape(block_rows, CLUSTERS, CL_ROWS)
        stored_scores = jnp.where(probed[:, :, None] & stored_live[None, :, :], stored_scores, masked_score)
        stored_best = lax.top_k(stored_scores, per_cluster)[0].reshape(block_rows, CLUSTERS * per_cluster)
        fresh_scores = jnp.einsum('bd,rd->br', query_f32, fresh, precision=lax.Precision.HIGHEST)
        fresh_scores = jnp.where(jnp.take(probed, item_places, axis=1), fresh_scores, masked_score)
        return lax.top_k(jnp.concatenate([stored_best, fresh_scores], 1), TOPK)[0]
    blocked_queries = queries.reshape(QUERIES // block_rows, block_rows, EMB)
    blocked_probes = probe_places.reshape(QUERIES // block_rows, block_rows, PROBES)
    return lax.map(score_block, (blocked_queries, blocked_probes)).reshape(QUERIES, TOPK)
```

```python
import jax
import jax.numpy as jnp
from jax import lax
from jax.sharding import PartitionSpec as P

TOPK = 128


masked_score = -1e30
unit_scale = 0.0625


def one_hot_take(table, index):
    ids = jnp.arange(table.shape[0], dtype=jnp.int32)
    hit = index[..., None] == ids
    return jnp.sum(jnp.where(hit, table, 0), axis=-1)


def body(
    item_feats,
    w_hidden,
    b_hidden,
    w_out,
    item_cluster,
    cluster_slot,
    catalog,
    cluster_fill,
    queries,
    probes,
):
    feat_count = lax.axis_size("feat")
    owner_count = lax.axis_size("clus")
    feat_index = lax.axis_index("feat")
    owner_index = lax.axis_index("clus")
    item_rows = item_feats.shape[0]
    device_rows = item_rows // feat_count

    pre_act = jnp.dot(
        lax.all_gather(item_feats, "feat", axis=1, tiled=True),
        w_hidden,
        preferred_element_type=jnp.float32,
    )
    hidden = jax.nn.silu(pre_act + b_hidden.astype(jnp.float32)).astype(jnp.bfloat16)
    projected = lax.psum_scatter(
        jnp.dot(hidden, w_out, preferred_element_type=jnp.float32),
        "feat",
        scatter_dimension=0,
        tiled=True,
    )
    scaling = lax.rsqrt(jnp.mean(projected * projected, axis=1, keepdims=True) + 1e-06) * unit_scale
    embedded = (projected * scaling).astype(jnp.bfloat16)
    emb_width = embedded.shape[1]

    my_clusters = lax.dynamic_slice_in_dim(item_cluster, feat_index * device_rows, device_rows, 0)
    my_places = one_hot_take(cluster_slot, my_clusters)
    owned_count = catalog.shape[0]
    target = my_places // owned_count
    capacity = 2 * device_rows // owner_count
    owner_hot = (target[:, None] == jnp.arange(owner_count, dtype=jnp.int32)[None, :]).astype(
        jnp.int32
    )
    before = jnp.cumsum(owner_hot, axis=0) - owner_hot
    position = jnp.sum(before * owner_hot, axis=1)
    send_slot = target * capacity + position
    slots = owner_count * capacity
    slot_hot = send_slot[None, :] == jnp.arange(slots, dtype=jnp.int32)[:, None]
    send_rows = jnp.dot(
        slot_hot.astype(jnp.bfloat16), embedded, preferred_element_type=jnp.float32
    ).astype(jnp.bfloat16)
    send_places = jnp.sum(jnp.where(slot_hot, my_places[None, :] + 1, 0), axis=1) - 1

    query_count = queries.shape[0]
    probe_count = probes.shape[1]
    probe_places = one_hot_take(cluster_slot, probes)
    probe_row = probe_places.reshape(-1, emb_width).astype(jnp.bfloat16)
    probe_lines = probe_row.shape[0]
    place_row = jnp.full((owner_count, emb_width), -1, jnp.int32)
    place_row = place_row.at[:, :capacity].set(send_places.reshape(owner_count, capacity))
    packed = jnp.concatenate(
        [
            jnp.broadcast_to(queries[None], (owner_count, query_count, emb_width)),
            jnp.broadcast_to(probe_row[None], (owner_count, probe_lines, emb_width)),
            send_rows.reshape(owner_count, capacity, emb_width),
            place_row.astype(jnp.bfloat16)[:, None, :],
        ],
        axis=1,
    )
    got = lax.all_to_all(packed, "clus", split_axis=0, concat_axis=0, tiled=True)
    at = 0
    all_queries = got[:, at : at + query_count].reshape(-1, emb_width)
    at += query_count
    all_probes = (
        got[:, at : at + probe_lines].astype(jnp.int32).reshape(owner_count * query_count, probe_count)
    )
    at += probe_lines
    got_rows = got[:, at : at + capacity].reshape(-1, emb_width)
    at += capacity
    got_places = got[:, at, :capacity].astype(jnp.int32).reshape(-1)

    row_dev = catalog.shape[1]
    first_owned = owner_index * owned_count
    local_ids = jnp.arange(owned_count, dtype=jnp.int32)
    owned_ids = first_owned + local_ids
    row_number = feat_index * row_dev + jnp.arange(row_dev, dtype=jnp.int32)
    stored_live = row_number[None, :] < cluster_fill[:, None]
    stored_owner = local_ids[:, None, None] == local_ids[None, None, :]
    stored_hot = (stored_owner & stored_live[:, :, None]).reshape(
        owned_count * row_dev, owned_count
    )
    fresh_local = got_places - first_owned
    fresh_hot = fresh_local[:, None] == local_ids[None, :]
    row_hot = jnp.concatenate([stored_hot, fresh_hot], 0).astype(jnp.float32)
    scored_rows = jnp.concatenate(
        [catalog.reshape(owned_count * row_dev, emb_width), got_rows], 0
    )
    probed = jnp.any(all_probes[:, :, None] == owned_ids[None, None, :], axis=1).astype(
        jnp.float32
    )
    allowed = jnp.einsum("bc,rc->br", probed, row_hot, precision=lax.Precision.HIGHEST) > 0.5
    scores = jnp.einsum("bd,rd->br", all_queries, scored_rows, preferred_element_type=jnp.float32)
    scores = jnp.where(allowed, scores, masked_score)
    local_best = lax.top_k(scores, TOPK)[0]

    arrived = lax.all_to_all(local_best, "clus", split_axis=0, concat_axis=1, tiled=True)
    narrowed = lax.top_k(arrived, TOPK)[0]
    gathered = lax.all_gather(narrowed, "feat", axis=1, tiled=True)
    return lax.top_k(gathered, TOPK)[0]


def solution(mesh):
    return jax.shard_map(
        body,
        mesh=mesh,
        in_specs=(
            P("clus", "feat"),
            P(None, "feat"),
            P("feat"),
            P("feat", None),
            P("clus"),
            P(),
            P("clus", "feat", None),
            P("clus"),
            P("clus", None),
            P("clus", None),
        ),
        out_specs=P("clus", None),
        check_vma=False,
    )
```

```python
import jax
import jax.numpy as jnp
from jax import lax
from jax.experimental import pallas as pl
from jax.experimental.pallas import tpu as pltpu
from jax.sharding import PartitionSpec as P

TOPK = 128


masked_score = -1e30
unit_scale = 0.0625
AXES = ("feat", "clus")

MESH = pl.DeviceIdType.MESH


def exchange(jobs, axes, sizes, collective_id):
    count = len(jobs)
    widest = max(sizes[axis] for _, axis, _ in jobs)
    used_axes = sorted({axis for _, axis, _ in jobs}, key=axes.index)
    shapes = []
    for x, axis, spread in jobs:
        shape = ((sizes[axis],) + x.shape) if spread else x.shape
        shapes.append(jax.ShapeDtypeStruct(shape, x.dtype))

    def kernel(*refs):
        ins, outs = refs[:count], refs[count : 2 * count]
        send_sem, recv_sem, own_sem = refs[2 * count :]
        where = {a: lax.axis_index(a) for a in axes}

        def device(axis, peer):
            return tuple(peer if a == axis else where[a] for a in axes)

        barrier = pltpu.get_barrier_semaphore()
        peers = 0
        for axis in used_axes:
            n = sizes[axis]
            for step in range(1, n):
                pl.semaphore_signal(
                    barrier,
                    inc=1,
                    device_id=device(axis, lax.rem(where[axis] + step, n)),
                    device_id_type=MESH,
                )
            peers += n - 1
        pl.semaphore_wait(barrier, peers)
        started = []
        locals_ = []
        for job, (x, axis, spread) in enumerate(jobs):
            n = sizes[axis]
            me = where[axis]
            src_of = (lambda d, job=job: ins[job]) if spread else (lambda d, job=job: ins[job].at[d])
            own = pltpu.make_async_copy(src_of(me), outs[job].at[me], own_sem.at[job])
            own.start()
            locals_.append(own)
            for step in range(1, n):
                peer = lax.rem(me + step, n)
                copy = pltpu.make_async_remote_copy(
                    src_ref=src_of(peer),
                    dst_ref=outs[job].at[me],
                    send_sem=send_sem.at[job, step],
                    recv_sem=recv_sem.at[job, step],
                    device_id=device(axis, peer),
                    device_id_type=MESH,
                )
                copy.start()
                started.append(copy)
        for copy in started:
            copy.wait_send()
        for copy in locals_:
            copy.wait()
        for job, (x, axis, spread) in enumerate(jobs):
            n = sizes[axis]
            me = where[axis]
            src_of = (lambda d, job=job: ins[job]) if spread else (lambda d, job=job: ins[job].at[d])
            for step in range(1, n):
                source = lax.rem(me + n - step, n)
                pltpu.make_async_copy(
                    src_of(source), outs[job].at[source], recv_sem.at[job, step]
                ).wait()

    return pl.pallas_call(
        kernel,
        out_shape=tuple(shapes),
        in_specs=[pl.BlockSpec(memory_space=pl.ANY)] * count,
        out_specs=tuple(pl.BlockSpec(memory_space=pl.ANY) for _ in jobs),
        scratch_shapes=[
            pltpu.SemaphoreType.DMA((count, widest)),
            pltpu.SemaphoreType.DMA((count, widest)),
            pltpu.SemaphoreType.DMA((count,)),
        ],
        compiler_params=pltpu.CompilerParams(collective_id=collective_id, has_side_effects=True),
    )(*[x for x, _, _ in jobs])


def one_hot_take(table, index):
    ids = jnp.arange(table.shape[0], dtype=jnp.int32)
    hit = index[..., None] == ids
    return jnp.sum(jnp.where(hit, table, 0), axis=-1)


def body(
    item_feats,
    w_hidden,
    b_hidden,
    w_out,
    item_cluster,
    cluster_slot,
    catalog,
    cluster_fill,
    queries,
    probes,
):
    feat_count = lax.axis_size("feat")
    owner_count = lax.axis_size("clus")
    sizes = {"feat": feat_count, "clus": owner_count}
    feat_index = lax.axis_index("feat")
    owner_index = lax.axis_index("clus")
    device_rows = item_feats.shape[0] // feat_count
    emb_width = queries.shape[1]
    owned_count, row_dev = catalog.shape[:2]
    query_count = queries.shape[0]
    probe_count = probes.shape[1]

    probe_places = one_hot_take(cluster_slot, probes)
    probe_row = probe_places.reshape(-1, emb_width).astype(jnp.bfloat16)
    probe_lines = probe_row.shape[0]
    asked = jnp.concatenate([queries, probe_row], axis=0)
    feats_all, asks = exchange(
        [(item_feats, "feat", True), (asked, "clus", True)], AXES, sizes, 0
    )

    feats = jnp.transpose(feats_all, (1, 0, 2)).reshape(feats_all.shape[1], -1)
    pre_act = jnp.dot(feats, w_hidden, preferred_element_type=jnp.float32)
    hidden = jax.nn.silu(pre_act + b_hidden.astype(jnp.float32)).astype(jnp.bfloat16)
    partial = jnp.dot(hidden, w_out, preferred_element_type=jnp.float32)
    (parts,) = exchange(
        [(partial.reshape(feat_count, device_rows, -1), "feat", False)], AXES, sizes, 1
    )
    projected = jnp.sum(parts, axis=0)
    scaling = lax.rsqrt(jnp.mean(projected * projected, axis=1, keepdims=True) + 1e-06) * unit_scale
    embedded = (projected * scaling).astype(jnp.bfloat16)

    my_clusters = lax.dynamic_slice_in_dim(item_cluster, feat_index * device_rows, device_rows, 0)
    my_places = one_hot_take(cluster_slot, my_clusters)
    target = my_places // owned_count
    capacity = 2 * device_rows // owner_count
    owner_hot = (target[:, None] == jnp.arange(owner_count, dtype=jnp.int32)[None, :]).astype(
        jnp.int32
    )
    before = jnp.cumsum(owner_hot, axis=0) - owner_hot
    position = jnp.sum(before * owner_hot, axis=1)
    send_slot = target * capacity + position
    slots = owner_count * capacity
    slot_hot = send_slot[None, :] == jnp.arange(slots, dtype=jnp.int32)[:, None]
    send_rows = jnp.dot(
        slot_hot.astype(jnp.bfloat16), embedded, preferred_element_type=jnp.float32
    ).astype(jnp.bfloat16)
    send_places = jnp.sum(jnp.where(slot_hot, my_places[None, :] + 1, 0), axis=1) - 1
    place_row = jnp.full((owner_count, emb_width), -1, jnp.int32)
    place_row = place_row.at[:, :capacity].set(send_places.reshape(owner_count, capacity))
    lines = (capacity + 1 + 7) // 8 * 8
    routed = jnp.concatenate(
        [
            send_rows.reshape(owner_count, capacity, emb_width),
            place_row.astype(jnp.bfloat16)[:, None, :],
            jnp.zeros((owner_count, lines - capacity - 1, emb_width), jnp.bfloat16),
        ],
        axis=1,
    )
    (got,) = exchange([(routed, "clus", False)], AXES, sizes, 2)
    got_rows = got[:, :capacity].reshape(-1, emb_width)
    got_places = got[:, capacity, :capacity].astype(jnp.int32).reshape(-1)
    all_queries = asks[:, :query_count].reshape(-1, emb_width)
    all_probes = (
        asks[:, query_count : query_count + probe_lines]
        .astype(jnp.int32)
        .reshape(owner_count * query_count, probe_count)
    )

    first_owned = owner_index * owned_count
    local_ids = jnp.arange(owned_count, dtype=jnp.int32)
    owned_ids = first_owned + local_ids
    row_number = feat_index * row_dev + jnp.arange(row_dev, dtype=jnp.int32)
    stored_live = row_number[None, :] < cluster_fill[:, None]
    probed = jnp.any(all_probes[:, :, None] == owned_ids[None, None, :], axis=1)
    stored_allowed = (probed[:, :, None] & stored_live[None]).reshape(-1, owned_count * row_dev)
    fresh_allowed = jnp.any(all_probes[:, :, None] == got_places[None, None, :], axis=1)
    allowed = jnp.concatenate([stored_allowed, fresh_allowed], axis=1)
    scored_rows = jnp.concatenate(
        [catalog.reshape(owned_count * row_dev, emb_width), got_rows], 0
    )
    scores = jnp.einsum("bd,rd->br", all_queries, scored_rows, preferred_element_type=jnp.float32)
    scores = jnp.where(allowed, scores, masked_score)
    local_best = lax.top_k(scores, TOPK)[0]

    (arrived,) = exchange(
        [(local_best.reshape(owner_count, query_count, -1), "clus", False)], AXES, sizes, 3
    )
    probe_owner = probe_places // owned_count
    earlier = jnp.arange(probe_count)[:, None] > jnp.arange(probe_count)[None, :]
    repeated = jnp.any(
        (probe_owner[:, :, None] == probe_owner[:, None, :]) & earlier[None], axis=2
    )
    owner_ids = jnp.arange(owner_count, dtype=jnp.int32)
    pick = probe_owner[:, :, None] == owner_ids[None, None, :]
    lists = jnp.transpose(arrived, (1, 0, 2))
    chosen = jnp.max(jnp.where(pick[..., None], lists[:, None], -jnp.inf), axis=2)
    chosen = jnp.where(repeated[..., None], masked_score, chosen)
    narrowed = lax.top_k(chosen.reshape(query_count, -1), TOPK)[0]
    (gathered,) = exchange([(narrowed, "feat", True)], AXES, sizes, 4)
    gathered = jnp.transpose(gathered, (1, 0, 2)).reshape(query_count, -1)
    return lax.top_k(gathered, TOPK)[0]


def solution(mesh):
    return jax.shard_map(
        body,
        mesh=mesh,
        in_specs=(
            P("clus", "feat"),
            P(None, "feat"),
            P("feat"),
            P("feat", None),
            P("clus"),
            P(),
            P("clus", "feat", None),
            P("clus"),
            P("clus", None),
            P("clus", None),
        ),
        out_specs=P("clus", None),
        check_vma=False,
    )
```

```python
import jax
import jax.numpy as jnp
from jax import lax
from jax.experimental import pallas as pl
from jax.experimental.pallas import tpu as pltpu
from jax.sharding import PartitionSpec as P

TOPK = 128


masked_score = -1e30
unit_scale = 0.0625
AXES = ("feat", "clus")

MESH = pl.DeviceIdType.MESH


def exchange(jobs, axes, sizes, collective_id):
    count = len(jobs)
    widest = max(sizes[axis] for _, axis, _ in jobs)
    used_axes = sorted({axis for _, axis, _ in jobs}, key=axes.index)
    shapes = []
    for x, axis, spread in jobs:
        shape = ((sizes[axis],) + x.shape) if spread else x.shape
        shapes.append(jax.ShapeDtypeStruct(shape, x.dtype))

    def kernel(*refs):
        ins, outs = refs[:count], refs[count : 2 * count]
        send_sem, recv_sem, own_sem = refs[2 * count :]
        where = {a: lax.axis_index(a) for a in axes}

        def device(axis, peer):
            return tuple(peer if a == axis else where[a] for a in axes)

        barrier = pltpu.get_barrier_semaphore()
        peers = 0
        for axis in used_axes:
            n = sizes[axis]
            for step in range(1, n):
                pl.semaphore_signal(
                    barrier,
                    inc=1,
                    device_id=device(axis, lax.rem(where[axis] + step, n)),
                    device_id_type=MESH,
                )
            peers += n - 1
        pl.semaphore_wait(barrier, peers)
        started = []
        locals_ = []
        for job, (x, axis, spread) in enumerate(jobs):
            n = sizes[axis]
            me = where[axis]
            src_of = (lambda d, job=job: ins[job]) if spread else (lambda d, job=job: ins[job].at[d])
            own = pltpu.make_async_copy(src_of(me), outs[job].at[me], own_sem.at[job])
            own.start()
            locals_.append(own)
            for step in range(1, n):
                peer = lax.rem(me + step, n)
                copy = pltpu.make_async_remote_copy(
                    src_ref=src_of(peer),
                    dst_ref=outs[job].at[me],
                    send_sem=send_sem.at[job, step],
                    recv_sem=recv_sem.at[job, step],
                    device_id=device(axis, peer),
                    device_id_type=MESH,
                )
                copy.start()
                started.append(copy)
        for copy in started:
            copy.wait_send()
        for copy in locals_:
            copy.wait()
        for job, (x, axis, spread) in enumerate(jobs):
            n = sizes[axis]
            me = where[axis]
            src_of = (lambda d, job=job: ins[job]) if spread else (lambda d, job=job: ins[job].at[d])
            for step in range(1, n):
                source = lax.rem(me + n - step, n)
                pltpu.make_async_copy(
                    src_of(source), outs[job].at[source], recv_sem.at[job, step]
                ).wait()

    return pl.pallas_call(
        kernel,
        out_shape=tuple(shapes),
        in_specs=[pl.BlockSpec(memory_space=pl.ANY)] * count,
        out_specs=tuple(pl.BlockSpec(memory_space=pl.ANY) for _ in jobs),
        scratch_shapes=[
            pltpu.SemaphoreType.DMA((count, widest)),
            pltpu.SemaphoreType.DMA((count, widest)),
            pltpu.SemaphoreType.DMA((count,)),
        ],
        compiler_params=pltpu.CompilerParams(collective_id=collective_id, has_side_effects=True),
    )(*[x for x, _, _ in jobs])


def compare_split(x, k, j):
    n = x.shape[0]
    tile = x.shape[1:]
    if k == 0:
        v = x.reshape((n // (2 * j), 2, j) + tile)
        a, b = v[:, 0], v[:, 1]
        return jnp.stack([jnp.maximum(a, b), jnp.minimum(a, b)], axis=1).reshape(x.shape)
    v = x.reshape((n // (2 * k), 2, k // (2 * j), 2, j) + tile)
    up_a, up_b = v[:, 0, :, 0], v[:, 0, :, 1]
    down_a, down_b = v[:, 1, :, 0], v[:, 1, :, 1]
    up = jnp.stack([jnp.minimum(up_a, up_b), jnp.maximum(up_a, up_b)], axis=2)
    down = jnp.stack([jnp.maximum(down_a, down_b), jnp.minimum(down_a, down_b)], axis=2)
    return jnp.stack([up, down], axis=1).reshape(x.shape)


def top_half_kernel(x_ref, o_ref):
    x = x_ref[...]
    n = x.shape[0]
    half = n // 2
    k = 2
    while k <= half:
        j = k // 2
        while j >= 1:
            x = compare_split(x, k, j)
            j //= 2
        k *= 2
    x = jnp.maximum(x[:half], x[half:])
    j = half // 2
    while j >= 1:
        x = compare_split(x, 0, j)
        j //= 2
    o_ref[...] = x


def top_half(x):
    n = x.shape[0]
    return pl.pallas_call(
        top_half_kernel,
        out_shape=jax.ShapeDtypeStruct((n // 2,) + x.shape[1:], x.dtype),
        in_specs=[pl.BlockSpec(memory_space=pltpu.VMEM)],
        out_specs=pl.BlockSpec(memory_space=pltpu.VMEM),
    )(x)


def one_hot_take(table, index):
    ids = jnp.arange(table.shape[0], dtype=jnp.int32)
    hit = index[..., None] == ids
    return jnp.sum(jnp.where(hit, table, 0), axis=-1)


def body(
    item_feats,
    w_hidden,
    b_hidden,
    w_out,
    item_cluster,
    cluster_slot,
    catalog,
    cluster_fill,
    queries,
    probes,
):
    feat_count = lax.axis_size("feat")
    owner_count = lax.axis_size("clus")
    sizes = {"feat": feat_count, "clus": owner_count}
    feat_index = lax.axis_index("feat")
    owner_index = lax.axis_index("clus")
    device_rows = item_feats.shape[0] // feat_count
    emb_width = queries.shape[1]
    owned_count, row_dev = catalog.shape[:2]
    query_count = queries.shape[0]
    probe_count = probes.shape[1]

    probe_places = one_hot_take(cluster_slot, probes)
    probe_row = probe_places.reshape(-1, emb_width).astype(jnp.bfloat16)
    probe_lines = probe_row.shape[0]
    asked = jnp.concatenate([queries, probe_row], axis=0)
    feats_all, asks = exchange(
        [(item_feats, "feat", True), (asked, "clus", True)], AXES, sizes, 0
    )

    feats = jnp.transpose(feats_all, (1, 0, 2)).reshape(feats_all.shape[1], -1)
    pre_act = jnp.dot(feats, w_hidden, preferred_element_type=jnp.float32)
    hidden = jax.nn.silu(pre_act + b_hidden.astype(jnp.float32)).astype(jnp.bfloat16)
    partial = jnp.dot(hidden, w_out, preferred_element_type=jnp.float32)
    (parts,) = exchange(
        [(partial.reshape(feat_count, device_rows, -1), "feat", False)], AXES, sizes, 1
    )
    projected = jnp.sum(parts, axis=0)
    scaling = lax.rsqrt(jnp.mean(projected * projected, axis=1, keepdims=True) + 1e-06) * unit_scale
    embedded = (projected * scaling).astype(jnp.bfloat16)

    my_clusters = lax.dynamic_slice_in_dim(item_cluster, feat_index * device_rows, device_rows, 0)
    my_places = one_hot_take(cluster_slot, my_clusters)
    target = my_places // owned_count
    capacity = 2 * device_rows // owner_count
    owner_hot = (target[:, None] == jnp.arange(owner_count, dtype=jnp.int32)[None, :]).astype(
        jnp.int32
    )
    before = jnp.cumsum(owner_hot, axis=0) - owner_hot
    position = jnp.sum(before * owner_hot, axis=1)
    send_slot = target * capacity + position
    slots = owner_count * capacity
    slot_hot = send_slot[None, :] == jnp.arange(slots, dtype=jnp.int32)[:, None]
    send_rows = jnp.dot(
        slot_hot.astype(jnp.bfloat16), embedded, preferred_element_type=jnp.float32
    ).astype(jnp.bfloat16)
    send_places = jnp.sum(jnp.where(slot_hot, my_places[None, :] + 1, 0), axis=1) - 1
    place_row = jnp.full((owner_count, emb_width), -1, jnp.int32)
    place_row = place_row.at[:, :capacity].set(send_places.reshape(owner_count, capacity))
    lines = (capacity + 1 + 7) // 8 * 8
    routed = jnp.concatenate(
        [
            send_rows.reshape(owner_count, capacity, emb_width),
            place_row.astype(jnp.bfloat16)[:, None, :],
            jnp.zeros((owner_count, lines - capacity - 1, emb_width), jnp.bfloat16),
        ],
        axis=1,
    )
    (got,) = exchange([(routed, "clus", False)], AXES, sizes, 2)
    got_rows = got[:, :capacity].reshape(-1, emb_width)
    got_places = got[:, capacity, :capacity].astype(jnp.int32).reshape(-1)
    all_queries = asks[:, :query_count].reshape(-1, emb_width)
    all_probes = (
        asks[:, query_count : query_count + probe_lines]
        .astype(jnp.int32)
        .reshape(owner_count * query_count, probe_count)
    )

    first_owned = owner_index * owned_count
    local_ids = jnp.arange(owned_count, dtype=jnp.int32)
    owned_ids = first_owned + local_ids
    row_number = feat_index * row_dev + jnp.arange(row_dev, dtype=jnp.int32)
    stored_live = row_number[None, :] < cluster_fill[:, None]
    probed = jnp.any(all_probes[:, :, None] == owned_ids[None, None, :], axis=1)
    stored_allowed = (jnp.transpose(probed)[:, None, :] & stored_live[:, :, None]).reshape(
        owned_count * row_dev, -1
    )
    fresh_allowed = jnp.any(
        got_places[:, None, None] == jnp.transpose(all_probes)[None, :, :], axis=1
    )
    allowed = jnp.concatenate([stored_allowed, fresh_allowed], axis=0)
    scored_rows = jnp.concatenate(
        [catalog.reshape(owned_count * row_dev, emb_width), got_rows], 0
    )
    scores = jnp.einsum("rd,bd->rb", scored_rows, all_queries, preferred_element_type=jnp.float32)
    scores = jnp.where(allowed, scores, masked_score)
    lanes = 128
    best = top_half(scores.reshape(scores.shape[0], -1, lanes))
    local_best = jnp.transpose(best.reshape(best.shape[0], -1))

    (arrived,) = exchange(
        [(local_best.reshape(owner_count, query_count, -1), "clus", False)], AXES, sizes, 3
    )
    probe_owner = probe_places // owned_count
    earlier = jnp.arange(probe_count)[:, None] > jnp.arange(probe_count)[None, :]
    repeated = jnp.any(
        (probe_owner[:, :, None] == probe_owner[:, None, :]) & earlier[None], axis=2
    )
    owner_ids = jnp.arange(owner_count, dtype=jnp.int32)
    pick = probe_owner[:, :, None] == owner_ids[None, None, :]
    lists = jnp.transpose(arrived, (1, 0, 2))
    chosen = jnp.max(jnp.where(pick[..., None], lists[:, None], -jnp.inf), axis=2)
    chosen = jnp.where(repeated[..., None], masked_score, chosen)
    narrowed = lax.top_k(chosen.reshape(query_count, -1), TOPK)[0]
    (gathered,) = exchange([(narrowed, "feat", True)], AXES, sizes, 4)
    gathered = jnp.transpose(gathered, (1, 0, 2)).reshape(query_count, -1)
    return lax.top_k(gathered, TOPK)[0]


def solution(mesh):
    return jax.shard_map(
        body,
        mesh=mesh,
        in_specs=(
            P("clus", "feat"),
            P(None, "feat"),
            P("feat"),
            P("feat", None),
            P("clus"),
            P(),
            P("clus", "feat", None),
            P("clus"),
            P("clus", None),
            P("clus", None),
        ),
        out_specs=P("clus", None),
        check_vma=False,
    )
```

```python
import jax
import jax.numpy as jnp
from jax import lax
from jax.experimental import pallas as pl
from jax.experimental.pallas import tpu as pltpu
from jax.sharding import PartitionSpec as P

TOPK = 128


masked_score = -1e30
unit_scale = 0.0625
AXES = ("feat", "clus")

MESH = pl.DeviceIdType.MESH


def exchange(jobs, axes, sizes, collective_id):
    count = len(jobs)
    widest = max(sizes[axis] for _, axis, _ in jobs)
    used_axes = sorted({axis for _, axis, _ in jobs}, key=axes.index)
    shapes = []
    for x, axis, spread in jobs:
        shape = ((sizes[axis],) + x.shape) if spread else x.shape
        shapes.append(jax.ShapeDtypeStruct(shape, x.dtype))

    def kernel(*refs):
        ins, outs = refs[:count], refs[count : 2 * count]
        send_sem, recv_sem, own_sem = refs[2 * count :]
        where = {a: lax.axis_index(a) for a in axes}

        def device(axis, peer):
            return tuple(peer if a == axis else where[a] for a in axes)

        barrier = pltpu.get_barrier_semaphore()
        peers = 0
        for axis in used_axes:
            n = sizes[axis]
            for step in range(1, n):
                pl.semaphore_signal(
                    barrier,
                    inc=1,
                    device_id=device(axis, lax.rem(where[axis] + step, n)),
                    device_id_type=MESH,
                )
            peers += n - 1
        pl.semaphore_wait(barrier, peers)
        started = []
        locals_ = []
        for job, (x, axis, spread) in enumerate(jobs):
            n = sizes[axis]
            me = where[axis]
            src_of = (lambda d, job=job: ins[job]) if spread else (lambda d, job=job: ins[job].at[d])
            own = pltpu.make_async_copy(src_of(me), outs[job].at[me], own_sem.at[job])
            own.start()
            locals_.append(own)
            for step in range(1, n):
                peer = lax.rem(me + step, n)
                copy = pltpu.make_async_remote_copy(
                    src_ref=src_of(peer),
                    dst_ref=outs[job].at[me],
                    send_sem=send_sem.at[job, step],
                    recv_sem=recv_sem.at[job, step],
                    device_id=device(axis, peer),
                    device_id_type=MESH,
                )
                copy.start()
                started.append(copy)
        for copy in started:
            copy.wait_send()
        for copy in locals_:
            copy.wait()
        for job, (x, axis, spread) in enumerate(jobs):
            n = sizes[axis]
            me = where[axis]
            src_of = (lambda d, job=job: ins[job]) if spread else (lambda d, job=job: ins[job].at[d])
            for step in range(1, n):
                source = lax.rem(me + n - step, n)
                pltpu.make_async_copy(
                    src_of(source), outs[job].at[source], recv_sem.at[job, step]
                ).wait()

    return pl.pallas_call(
        kernel,
        out_shape=tuple(shapes),
        in_specs=[pl.BlockSpec(memory_space=pl.ANY)] * count,
        out_specs=tuple(pl.BlockSpec(memory_space=pl.ANY) for _ in jobs),
        scratch_shapes=[
            pltpu.SemaphoreType.DMA((count, widest)),
            pltpu.SemaphoreType.DMA((count, widest)),
            pltpu.SemaphoreType.DMA((count,)),
        ],
        compiler_params=pltpu.CompilerParams(collective_id=collective_id, has_side_effects=True),
    )(*[x for x, _, _ in jobs])


def compare_split(x, k, j):
    n = x.shape[0]
    tile = x.shape[1:]
    if k == 0:
        v = x.reshape((n // (2 * j), 2, j) + tile)
        a, b = v[:, 0], v[:, 1]
        return jnp.stack([jnp.maximum(a, b), jnp.minimum(a, b)], axis=1).reshape(x.shape)
    v = x.reshape((n // (2 * k), 2, k // (2 * j), 2, j) + tile)
    up_a, up_b = v[:, 0, :, 0], v[:, 0, :, 1]
    down_a, down_b = v[:, 1, :, 0], v[:, 1, :, 1]
    up = jnp.stack([jnp.minimum(up_a, up_b), jnp.maximum(up_a, up_b)], axis=2)
    down = jnp.stack([jnp.maximum(down_a, down_b), jnp.minimum(down_a, down_b)], axis=2)
    return jnp.stack([up, down], axis=1).reshape(x.shape)


def top_half_kernel(x_ref, o_ref):
    x = x_ref[...]
    n = x.shape[0]
    half = n // 2
    k = 2
    while k <= half:
        j = k // 2
        while j >= 1:
            x = compare_split(x, k, j)
            j //= 2
        k *= 2
    x = jnp.maximum(x[:half], x[half:])
    j = half // 2
    while j >= 1:
        x = compare_split(x, 0, j)
        j //= 2
    o_ref[...] = x


def top_half(x):
    n = x.shape[0]
    return pl.pallas_call(
        top_half_kernel,
        out_shape=jax.ShapeDtypeStruct((n // 2,) + x.shape[1:], x.dtype),
        in_specs=[pl.BlockSpec(memory_space=pltpu.VMEM)],
        out_specs=pl.BlockSpec(memory_space=pltpu.VMEM),
    )(x)


def one_hot_take(table, index):
    ids = jnp.arange(table.shape[0], dtype=jnp.int32)
    hit = index[..., None] == ids
    return jnp.sum(jnp.where(hit, table, 0), axis=-1)


def body(
    item_feats,
    w_hidden,
    b_hidden,
    w_out,
    item_cluster,
    cluster_slot,
    catalog,
    cluster_fill,
    queries,
    probes,
):
    feat_count = lax.axis_size("feat")
    owner_count = lax.axis_size("clus")
    sizes = {"feat": feat_count, "clus": owner_count}
    feat_index = lax.axis_index("feat")
    owner_index = lax.axis_index("clus")
    device_rows = item_feats.shape[0] // feat_count
    emb_width = queries.shape[1]
    owned_count, row_dev = catalog.shape[:2]
    query_count = queries.shape[0]
    probe_count = probes.shape[1]

    probe_places = one_hot_take(cluster_slot, probes)
    probe_row = probe_places.reshape(-1, emb_width).astype(jnp.bfloat16)
    probe_lines = probe_row.shape[0]
    share = query_count // feat_count
    asked = jnp.concatenate(
        [lax.dynamic_slice_in_dim(queries, feat_index * share, share, 0), probe_row], axis=0
    )
    feats_all, asks = exchange(
        [(item_feats, "feat", True), (asked, "clus", True)], AXES, sizes, 0
    )

    feats = jnp.transpose(feats_all, (1, 0, 2)).reshape(feats_all.shape[1], -1)
    pre_act = jnp.dot(feats, w_hidden, preferred_element_type=jnp.float32)
    hidden = jax.nn.silu(pre_act + b_hidden.astype(jnp.float32)).astype(jnp.bfloat16)
    partial = jnp.dot(hidden, w_out, preferred_element_type=jnp.float32)
    (parts,) = exchange(
        [(partial.reshape(feat_count, device_rows, -1), "feat", False)], AXES, sizes, 1
    )
    projected = jnp.sum(parts, axis=0)
    scaling = lax.rsqrt(jnp.mean(projected * projected, axis=1, keepdims=True) + 1e-06) * unit_scale
    embedded = (projected * scaling).astype(jnp.bfloat16)

    my_clusters = lax.dynamic_slice_in_dim(item_cluster, feat_index * device_rows, device_rows, 0)
    my_places = one_hot_take(cluster_slot, my_clusters)
    target = my_places // owned_count
    capacity = 2 * device_rows // owner_count
    owner_hot = (target[:, None] == jnp.arange(owner_count, dtype=jnp.int32)[None, :]).astype(
        jnp.int32
    )
    before = jnp.cumsum(owner_hot, axis=0) - owner_hot
    position = jnp.sum(before * owner_hot, axis=1)
    send_slot = target * capacity + position
    slots = owner_count * capacity
    slot_hot = send_slot[None, :] == jnp.arange(slots, dtype=jnp.int32)[:, None]
    send_rows = jnp.dot(
        slot_hot.astype(jnp.bfloat16), embedded, preferred_element_type=jnp.float32
    ).astype(jnp.bfloat16)
    send_places = jnp.sum(jnp.where(slot_hot, my_places[None, :] + 1, 0), axis=1) - 1
    place_row = jnp.full((owner_count, emb_width), -1, jnp.int32)
    place_row = place_row.at[:, :capacity].set(send_places.reshape(owner_count, capacity))
    lines = (capacity + 1 + 7) // 8 * 8
    routed = jnp.concatenate(
        [
            send_rows.reshape(owner_count, capacity, emb_width),
            place_row.astype(jnp.bfloat16)[:, None, :],
            jnp.zeros((owner_count, lines - capacity - 1, emb_width), jnp.bfloat16),
        ],
        axis=1,
    )
    got, spread = exchange([(routed, "clus", False), (asks, "feat", True)], AXES, sizes, 2)
    got_rows = got[:, :capacity].reshape(-1, emb_width)
    got_places = got[:, capacity, :capacity].astype(jnp.int32).reshape(-1)
    all_queries = spread[:, :, :share].reshape(-1, emb_width)
    all_probes = (
        spread[0, :, share : share + probe_lines]
        .astype(jnp.int32)
        .reshape(owner_count, feat_count, share, probe_count)
    )
    all_probes = jnp.transpose(all_probes, (1, 0, 2, 3)).reshape(-1, probe_count)

    first_owned = owner_index * owned_count
    local_ids = jnp.arange(owned_count, dtype=jnp.int32)
    owned_ids = first_owned + local_ids
    row_number = feat_index * row_dev + jnp.arange(row_dev, dtype=jnp.int32)
    stored_live = row_number[None, :] < cluster_fill[:, None]
    probed = jnp.any(all_probes[:, :, None] == owned_ids[None, None, :], axis=1)
    stored_allowed = (jnp.transpose(probed)[:, None, :] & stored_live[:, :, None]).reshape(
        owned_count * row_dev, -1
    )
    fresh_allowed = jnp.any(
        got_places[:, None, None] == jnp.transpose(all_probes)[None, :, :], axis=1
    )
    allowed = jnp.concatenate([stored_allowed, fresh_allowed], axis=0)
    scored_rows = jnp.concatenate(
        [catalog.reshape(owned_count * row_dev, emb_width), got_rows], 0
    )
    scores = jnp.einsum("rd,bd->rb", scored_rows, all_queries, preferred_element_type=jnp.float32)
    scores = jnp.where(allowed, scores, masked_score)
    lanes = 128
    best = top_half(scores.reshape(scores.shape[0], -1, lanes))
    local_best = jnp.transpose(
        best.reshape(best.shape[0], feat_count, owner_count, share), (2, 1, 3, 0)
    )

    (arrived,) = exchange(
        [(local_best.reshape(owner_count, query_count, -1), "clus", False)], AXES, sizes, 3
    )
    probe_owner = probe_places // owned_count
    earlier = jnp.arange(probe_count)[:, None] > jnp.arange(probe_count)[None, :]
    repeated = jnp.any(
        (probe_owner[:, :, None] == probe_owner[:, None, :]) & earlier[None], axis=2
    )
    owner_ids = jnp.arange(owner_count, dtype=jnp.int32)
    pick = probe_owner[:, :, None] == owner_ids[None, None, :]
    lists = jnp.transpose(arrived, (1, 0, 2))
    chosen = jnp.max(jnp.where(pick[..., None], lists[:, None], -jnp.inf), axis=2)
    chosen = jnp.where(repeated[..., None], masked_score, chosen)
    narrowed = lax.top_k(chosen.reshape(query_count, -1), TOPK)[0]
    (gathered,) = exchange([(narrowed, "feat", True)], AXES, sizes, 4)
    gathered = jnp.transpose(gathered, (1, 0, 2)).reshape(query_count, -1)
    return lax.top_k(gathered, TOPK)[0]


def solution(mesh):
    return jax.shard_map(
        body,
        mesh=mesh,
        in_specs=(
            P("clus", "feat"),
            P(None, "feat"),
            P("feat"),
            P("feat", None),
            P("clus"),
            P(),
            P("clus", "feat", None),
            P("clus"),
            P("clus", None),
            P("clus", None),
        ),
        out_specs=P("clus", None),
        check_vma=False,
    )
```

```python
import jax
import jax.numpy as jnp
from jax import lax
from jax.experimental import pallas as pl
from jax.experimental.pallas import tpu as pltpu
from jax.sharding import PartitionSpec as P

TOPK = 128


masked_score = -1e30
unit_scale = 0.0625
AXES = ("feat", "clus")

MESH = pl.DeviceIdType.MESH


def exchange(jobs, axes, sizes, collective_id):
    count = len(jobs)
    widest = max(sizes[axis] for _, axis, _ in jobs)
    used_axes = sorted({axis for _, axis, _ in jobs}, key=axes.index)
    shapes = []
    for x, axis, spread in jobs:
        shape = ((sizes[axis],) + x.shape) if spread else x.shape
        shapes.append(jax.ShapeDtypeStruct(shape, x.dtype))

    def kernel(*refs):
        ins, outs = refs[:count], refs[count : 2 * count]
        send_sem, recv_sem, own_sem = refs[2 * count :]
        where = {a: lax.axis_index(a) for a in axes}

        def device(axis, peer):
            return tuple(peer if a == axis else where[a] for a in axes)

        barrier = pltpu.get_barrier_semaphore()
        peers = 0
        for axis in used_axes:
            n = sizes[axis]
            for step in range(1, n):
                pl.semaphore_signal(
                    barrier,
                    inc=1,
                    device_id=device(axis, lax.rem(where[axis] + step, n)),
                    device_id_type=MESH,
                )
            peers += n - 1
        pl.semaphore_wait(barrier, peers)
        started = []
        locals_ = []
        for job, (x, axis, spread) in enumerate(jobs):
            n = sizes[axis]
            me = where[axis]
            src_of = (lambda d, job=job: ins[job]) if spread else (lambda d, job=job: ins[job].at[d])
            own = pltpu.make_async_copy(src_of(me), outs[job].at[me], own_sem.at[job])
            own.start()
            locals_.append(own)
            for step in range(1, n):
                peer = lax.rem(me + step, n)
                copy = pltpu.make_async_remote_copy(
                    src_ref=src_of(peer),
                    dst_ref=outs[job].at[me],
                    send_sem=send_sem.at[job, step],
                    recv_sem=recv_sem.at[job, step],
                    device_id=device(axis, peer),
                    device_id_type=MESH,
                )
                copy.start()
                started.append(copy)
        for copy in started:
            copy.wait_send()
        for copy in locals_:
            copy.wait()
        for job, (x, axis, spread) in enumerate(jobs):
            n = sizes[axis]
            me = where[axis]
            src_of = (lambda d, job=job: ins[job]) if spread else (lambda d, job=job: ins[job].at[d])
            for step in range(1, n):
                source = lax.rem(me + n - step, n)
                pltpu.make_async_copy(
                    src_of(source), outs[job].at[source], recv_sem.at[job, step]
                ).wait()

    return pl.pallas_call(
        kernel,
        out_shape=tuple(shapes),
        in_specs=[pl.BlockSpec(memory_space=pl.ANY)] * count,
        out_specs=tuple(pl.BlockSpec(memory_space=pl.ANY) for _ in jobs),
        scratch_shapes=[
            pltpu.SemaphoreType.DMA((count, widest)),
            pltpu.SemaphoreType.DMA((count, widest)),
            pltpu.SemaphoreType.DMA((count,)),
        ],
        compiler_params=pltpu.CompilerParams(collective_id=collective_id, has_side_effects=True),
    )(*[x for x, _, _ in jobs])


def compare_split(x, k, j):
    n = x.shape[0]
    tile = x.shape[1:]
    if k == 0:
        v = x.reshape((n // (2 * j), 2, j) + tile)
        a, b = v[:, 0], v[:, 1]
        return jnp.stack([jnp.maximum(a, b), jnp.minimum(a, b)], axis=1).reshape(x.shape)
    v = x.reshape((n // (2 * k), 2, k // (2 * j), 2, j) + tile)
    up_a, up_b = v[:, 0, :, 0], v[:, 0, :, 1]
    down_a, down_b = v[:, 1, :, 0], v[:, 1, :, 1]
    up = jnp.stack([jnp.minimum(up_a, up_b), jnp.maximum(up_a, up_b)], axis=2)
    down = jnp.stack([jnp.maximum(down_a, down_b), jnp.minimum(down_a, down_b)], axis=2)
    return jnp.stack([up, down], axis=1).reshape(x.shape)


def top_half_kernel(x_ref, o_ref):
    x = x_ref[...]
    n = x.shape[0]
    half = n // 2
    k = 2
    while k <= half:
        j = k // 2
        while j >= 1:
            x = compare_split(x, k, j)
            j //= 2
        k *= 2
    x = jnp.maximum(x[:half], x[half:])
    j = half // 2
    while j >= 1:
        x = compare_split(x, 0, j)
        j //= 2
    o_ref[...] = x


def top_half(x):
    n = x.shape[0]
    return pl.pallas_call(
        top_half_kernel,
        out_shape=jax.ShapeDtypeStruct((n // 2,) + x.shape[1:], x.dtype),
        in_specs=[pl.BlockSpec(memory_space=pltpu.VMEM)],
        out_specs=pl.BlockSpec(memory_space=pltpu.VMEM),
    )(x)


def one_hot_take(table, index):
    ids = jnp.arange(table.shape[0], dtype=jnp.int32)
    hit = index[..., None] == ids
    return jnp.sum(jnp.where(hit, table, 0), axis=-1)


def body(
    item_feats,
    w_hidden,
    b_hidden,
    w_out,
    item_cluster,
    cluster_slot,
    catalog,
    cluster_fill,
    queries,
    probes,
):
    feat_count = lax.axis_size("feat")
    owner_count = lax.axis_size("clus")
    sizes = {"feat": feat_count, "clus": owner_count}
    feat_index = lax.axis_index("feat")
    owner_index = lax.axis_index("clus")
    device_rows = item_feats.shape[0] // feat_count
    emb_width = queries.shape[1]
    owned_count, row_dev = catalog.shape[:2]
    query_count = queries.shape[0]
    probe_count = probes.shape[1]

    probe_places = one_hot_take(cluster_slot, probes)
    probe_row = probe_places.reshape(-1, emb_width).astype(jnp.bfloat16)
    probe_lines = probe_row.shape[0]
    asked = jnp.concatenate([queries, probe_row], axis=0)
    lanes = 128
    feats_all, asks = exchange(
        [(item_feats.reshape(-1, lanes), "feat", True), (asked, "clus", True)], AXES, sizes, 0
    )

    feats_all = feats_all.reshape((feat_count,) + item_feats.shape)
    feats = jnp.transpose(feats_all, (1, 0, 2)).reshape(feats_all.shape[1], -1)
    pre_act = jnp.dot(feats, w_hidden, preferred_element_type=jnp.float32)
    hidden = jax.nn.silu(pre_act + b_hidden.astype(jnp.float32)).astype(jnp.bfloat16)
    partial = jnp.dot(hidden, w_out, preferred_element_type=jnp.float32)
    (parts,) = exchange(
        [(partial.reshape(feat_count, device_rows, -1), "feat", False)], AXES, sizes, 1
    )
    projected = jnp.sum(parts, axis=0)
    scaling = lax.rsqrt(jnp.mean(projected * projected, axis=1, keepdims=True) + 1e-06) * unit_scale
    embedded = (projected * scaling).astype(jnp.bfloat16)

    my_clusters = lax.dynamic_slice_in_dim(item_cluster, feat_index * device_rows, device_rows, 0)
    my_places = one_hot_take(cluster_slot, my_clusters)
    target = my_places // owned_count
    capacity = 2 * device_rows // owner_count
    owner_hot = (target[:, None] == jnp.arange(owner_count, dtype=jnp.int32)[None, :]).astype(
        jnp.int32
    )
    before = jnp.cumsum(owner_hot, axis=0) - owner_hot
    position = jnp.sum(before * owner_hot, axis=1)
    send_slot = target * capacity + position
    slots = owner_count * capacity
    slot_hot = send_slot[None, :] == jnp.arange(slots, dtype=jnp.int32)[:, None]
    send_rows = jnp.dot(
        slot_hot.astype(jnp.bfloat16), embedded, preferred_element_type=jnp.float32
    ).astype(jnp.bfloat16)
    send_places = jnp.sum(jnp.where(slot_hot, my_places[None, :] + 1, 0), axis=1) - 1
    place_row = jnp.full((owner_count, emb_width), -1, jnp.int32)
    place_row = place_row.at[:, :capacity].set(send_places.reshape(owner_count, capacity))
    lines = (capacity + 1 + 7) // 8 * 8
    routed = jnp.concatenate(
        [
            send_rows.reshape(owner_count, capacity, emb_width),
            place_row.astype(jnp.bfloat16)[:, None, :],
            jnp.zeros((owner_count, lines - capacity - 1, emb_width), jnp.bfloat16),
        ],
        axis=1,
    )
    (got,) = exchange([(routed, "clus", False)], AXES, sizes, 2)
    got_rows = got[:, :capacity].reshape(-1, emb_width)
    got_places = got[:, capacity, :capacity].astype(jnp.int32).reshape(-1)
    all_queries = asks[:, :query_count].reshape(-1, emb_width)
    all_probes = (
        asks[:, query_count : query_count + probe_lines]
        .astype(jnp.int32)
        .reshape(owner_count * query_count, probe_count)
    )

    first_owned = owner_index * owned_count
    local_ids = jnp.arange(owned_count, dtype=jnp.int32)
    owned_ids = first_owned + local_ids
    row_number = feat_index * row_dev + jnp.arange(row_dev, dtype=jnp.int32)
    stored_live = row_number[None, :] < cluster_fill[:, None]
    probed = jnp.any(all_probes[:, :, None] == owned_ids[None, None, :], axis=1)
    stored_allowed = (jnp.transpose(probed)[:, None, :] & stored_live[:, :, None]).reshape(
        owned_count * row_dev, -1
    )
    fresh_allowed = jnp.any(
        got_places[:, None, None] == jnp.transpose(all_probes)[None, :, :], axis=1
    )
    allowed = jnp.concatenate([stored_allowed, fresh_allowed], axis=0)
    scored_rows = jnp.concatenate(
        [catalog.reshape(owned_count * row_dev, emb_width), got_rows], 0
    )
    scores = jnp.einsum("rd,bd->rb", scored_rows, all_queries, preferred_element_type=jnp.float32)
    scores = jnp.where(allowed, scores, masked_score)
    lanes = 128
    best = top_half(scores.reshape(scores.shape[0], -1, lanes))
    local_best = jnp.transpose(best.reshape(best.shape[0], -1))

    (arrived,) = exchange(
        [(local_best.reshape(owner_count, query_count, -1), "clus", False)], AXES, sizes, 3
    )
    probe_owner = probe_places // owned_count
    earlier = jnp.arange(probe_count)[:, None] > jnp.arange(probe_count)[None, :]
    repeated = jnp.any(
        (probe_owner[:, :, None] == probe_owner[:, None, :]) & earlier[None], axis=2
    )
    owner_ids = jnp.arange(owner_count, dtype=jnp.int32)
    pick = probe_owner[:, :, None] == owner_ids[None, None, :]
    lists = jnp.transpose(arrived, (1, 0, 2))
    chosen = jnp.max(jnp.where(pick[..., None], lists[:, None], -jnp.inf), axis=2)
    chosen = jnp.where(repeated[..., None], masked_score, chosen)
    narrowed = lax.top_k(chosen.reshape(query_count, -1), TOPK)[0]
    (gathered,) = exchange([(narrowed, "feat", True)], AXES, sizes, 4)
    gathered = jnp.transpose(gathered, (1, 0, 2)).reshape(query_count, -1)
    return lax.top_k(gathered, TOPK)[0]


def solution(mesh):
    return jax.shard_map(
        body,
        mesh=mesh,
        in_specs=(
            P("clus", "feat"),
            P(None, "feat"),
            P("feat"),
            P("feat", None),
            P("clus"),
            P(),
            P("clus", "feat", None),
            P("clus"),
            P("clus", None),
            P("clus", None),
        ),
        out_specs=P("clus", None),
        check_vma=False,
    )
```

```python
import jax
import jax.numpy as jnp
from jax import lax
from jax.experimental import pallas as pl
from jax.experimental.pallas import tpu as pltpu
from jax.sharding import PartitionSpec as P

TOPK = 128


masked_score = -1e30
unit_scale = 0.0625
AXES = ("feat", "clus")

MESH = pl.DeviceIdType.MESH


def exchange(jobs, axes, sizes, collective_id):
    count = len(jobs)
    widest = max(sizes[axis] for _, axis, _ in jobs)
    used_axes = sorted({axis for _, axis, _ in jobs}, key=axes.index)
    shapes = []
    for x, axis, spread in jobs:
        shape = ((sizes[axis],) + x.shape) if spread else x.shape
        shapes.append(jax.ShapeDtypeStruct(shape, x.dtype))

    def kernel(*refs):
        ins, outs = refs[:count], refs[count : 2 * count]
        send_sem, recv_sem, own_sem = refs[2 * count :]
        where = {a: lax.axis_index(a) for a in axes}

        def device(axis, peer):
            return tuple(peer if a == axis else where[a] for a in axes)

        barrier = pltpu.get_barrier_semaphore()
        peers = 0
        for axis in used_axes:
            n = sizes[axis]
            for step in range(1, n):
                pl.semaphore_signal(
                    barrier,
                    inc=1,
                    device_id=device(axis, lax.rem(where[axis] + step, n)),
                    device_id_type=MESH,
                )
            peers += n - 1
        pl.semaphore_wait(barrier, peers)
        started = []
        locals_ = []
        for job, (x, axis, spread) in enumerate(jobs):
            n = sizes[axis]
            me = where[axis]
            src_of = (lambda d, job=job: ins[job]) if spread else (lambda d, job=job: ins[job].at[d])
            own = pltpu.make_async_copy(src_of(me), outs[job].at[me], own_sem.at[job])
            own.start()
            locals_.append(own)
            for step in range(1, n):
                peer = lax.rem(me + step, n)
                copy = pltpu.make_async_remote_copy(
                    src_ref=src_of(peer),
                    dst_ref=outs[job].at[me],
                    send_sem=send_sem.at[job, step],
                    recv_sem=recv_sem.at[job, step],
                    device_id=device(axis, peer),
                    device_id_type=MESH,
                )
                copy.start()
                started.append(copy)
        for copy in started:
            copy.wait_send()
        for copy in locals_:
            copy.wait()
        for job, (x, axis, spread) in enumerate(jobs):
            n = sizes[axis]
            me = where[axis]
            src_of = (lambda d, job=job: ins[job]) if spread else (lambda d, job=job: ins[job].at[d])
            for step in range(1, n):
                source = lax.rem(me + n - step, n)
                pltpu.make_async_copy(
                    src_of(source), outs[job].at[source], recv_sem.at[job, step]
                ).wait()

    return pl.pallas_call(
        kernel,
        out_shape=tuple(shapes),
        in_specs=[pl.BlockSpec(memory_space=pl.ANY)] * count,
        out_specs=tuple(pl.BlockSpec(memory_space=pl.ANY) for _ in jobs),
        scratch_shapes=[
            pltpu.SemaphoreType.DMA((count, widest)),
            pltpu.SemaphoreType.DMA((count, widest)),
            pltpu.SemaphoreType.DMA((count,)),
        ],
        compiler_params=pltpu.CompilerParams(collective_id=collective_id, has_side_effects=True),
    )(*[x for x, _, _ in jobs])


def compare_split(x, k, j):
    n = x.shape[0]
    tile = x.shape[1:]
    if k == 0:
        v = x.reshape((n // (2 * j), 2, j) + tile)
        a, b = v[:, 0], v[:, 1]
        return jnp.stack([jnp.maximum(a, b), jnp.minimum(a, b)], axis=1).reshape(x.shape)
    v = x.reshape((n // (2 * k), 2, k // (2 * j), 2, j) + tile)
    up_a, up_b = v[:, 0, :, 0], v[:, 0, :, 1]
    down_a, down_b = v[:, 1, :, 0], v[:, 1, :, 1]
    up = jnp.stack([jnp.minimum(up_a, up_b), jnp.maximum(up_a, up_b)], axis=2)
    down = jnp.stack([jnp.maximum(down_a, down_b), jnp.minimum(down_a, down_b)], axis=2)
    return jnp.stack([up, down], axis=1).reshape(x.shape)


def top_half_kernel(x_ref, o_ref):
    x = x_ref[...]
    n = x.shape[0]
    half = n // 2
    k = 2
    while k <= half:
        j = k // 2
        while j >= 1:
            x = compare_split(x, k, j)
            j //= 2
        k *= 2
    x = jnp.maximum(x[:half], x[half:])
    j = half // 2
    while j >= 1:
        x = compare_split(x, 0, j)
        j //= 2
    o_ref[...] = x


def top_half(x):
    n = x.shape[0]
    return pl.pallas_call(
        top_half_kernel,
        out_shape=jax.ShapeDtypeStruct((n // 2,) + x.shape[1:], x.dtype),
        in_specs=[pl.BlockSpec(memory_space=pltpu.VMEM)],
        out_specs=pl.BlockSpec(memory_space=pltpu.VMEM),
    )(x)


def one_hot_take(table, index):
    ids = jnp.arange(table.shape[0], dtype=jnp.int32)
    hit = index[..., None] == ids
    return jnp.sum(jnp.where(hit, table, 0), axis=-1)


def body(
    item_feats,
    w_hidden,
    b_hidden,
    w_out,
    item_cluster,
    cluster_slot,
    catalog,
    cluster_fill,
    queries,
    probes,
):
    feat_count = lax.axis_size("feat")
    owner_count = lax.axis_size("clus")
    sizes = {"feat": feat_count, "clus": owner_count}
    feat_index = lax.axis_index("feat")
    owner_index = lax.axis_index("clus")
    device_rows = item_feats.shape[0] // feat_count
    emb_width = queries.shape[1]
    owned_count, row_dev = catalog.shape[:2]
    query_count = queries.shape[0]
    probe_count = probes.shape[1]

    probe_places = one_hot_take(cluster_slot, probes)
    probe_row = probe_places.reshape(-1, emb_width).astype(jnp.bfloat16)
    probe_lines = probe_row.shape[0]
    asked = jnp.concatenate([queries, probe_row], axis=0)
    lanes = 128
    asks, feats_all = exchange(
        [(asked, "clus", True), (item_feats.reshape(-1, lanes), "feat", True)], AXES, sizes, 0
    )

    feats_all = feats_all.reshape((feat_count,) + item_feats.shape)
    feats = jnp.transpose(feats_all, (1, 0, 2)).reshape(feats_all.shape[1], -1)
    pre_act = jnp.dot(feats, w_hidden, preferred_element_type=jnp.float32)
    hidden = jax.nn.silu(pre_act + b_hidden.astype(jnp.float32)).astype(jnp.bfloat16)
    partial = jnp.dot(hidden, w_out, preferred_element_type=jnp.float32)
    (parts,) = exchange(
        [(partial.reshape(feat_count, device_rows, -1), "feat", False)], AXES, sizes, 1
    )
    projected = jnp.sum(parts, axis=0)
    scaling = lax.rsqrt(jnp.mean(projected * projected, axis=1, keepdims=True) + 1e-06) * unit_scale
    embedded = (projected * scaling).astype(jnp.bfloat16)

    my_clusters = lax.dynamic_slice_in_dim(item_cluster, feat_index * device_rows, device_rows, 0)
    my_places = one_hot_take(cluster_slot, my_clusters)
    target = my_places // owned_count
    capacity = 2 * device_rows // owner_count
    owner_hot = (target[:, None] == jnp.arange(owner_count, dtype=jnp.int32)[None, :]).astype(
        jnp.int32
    )
    before = jnp.cumsum(owner_hot, axis=0) - owner_hot
    position = jnp.sum(before * owner_hot, axis=1)
    send_slot = target * capacity + position
    slots = owner_count * capacity
    slot_hot = send_slot[None, :] == jnp.arange(slots, dtype=jnp.int32)[:, None]
    send_rows = jnp.dot(
        slot_hot.astype(jnp.bfloat16), embedded, preferred_element_type=jnp.float32
    ).astype(jnp.bfloat16)
    send_places = jnp.sum(jnp.where(slot_hot, my_places[None, :] + 1, 0), axis=1) - 1
    place_row = jnp.full((owner_count, emb_width), -1, jnp.int32)
    place_row = place_row.at[:, :capacity].set(send_places.reshape(owner_count, capacity))
    lines = (capacity + 1 + 7) // 8 * 8
    routed = jnp.concatenate(
        [
            send_rows.reshape(owner_count, capacity, emb_width),
            place_row.astype(jnp.bfloat16)[:, None, :],
            jnp.zeros((owner_count, lines - capacity - 1, emb_width), jnp.bfloat16),
        ],
        axis=1,
    )
    (got,) = exchange([(routed, "clus", False)], AXES, sizes, 2)
    got_rows = got[:, :capacity].reshape(-1, emb_width)
    got_places = got[:, capacity, :capacity].astype(jnp.int32).reshape(-1)
    all_queries = asks[:, :query_count].reshape(-1, emb_width)
    all_probes = (
        asks[:, query_count : query_count + probe_lines]
        .astype(jnp.int32)
        .reshape(owner_count * query_count, probe_count)
    )

    first_owned = owner_index * owned_count
    local_ids = jnp.arange(owned_count, dtype=jnp.int32)
    owned_ids = first_owned + local_ids
    row_number = feat_index * row_dev + jnp.arange(row_dev, dtype=jnp.int32)
    stored_live = row_number[None, :] < cluster_fill[:, None]
    probed = jnp.any(all_probes[:, :, None] == owned_ids[None, None, :], axis=1)
    stored_allowed = (jnp.transpose(probed)[:, None, :] & stored_live[:, :, None]).reshape(
        owned_count * row_dev, -1
    )
    fresh_allowed = jnp.any(
        got_places[:, None, None] == jnp.transpose(all_probes)[None, :, :], axis=1
    )
    allowed = jnp.concatenate([stored_allowed, fresh_allowed], axis=0)
    scored_rows = jnp.concatenate(
        [catalog.reshape(owned_count * row_dev, emb_width), got_rows], 0
    )
    scores = jnp.einsum("rd,bd->rb", scored_rows, all_queries, preferred_element_type=jnp.float32)
    scores = jnp.where(allowed, scores, masked_score)
    lanes = 128
    best = top_half(scores.reshape(scores.shape[0], -1, lanes))
    local_best = jnp.transpose(best.reshape(best.shape[0], -1))

    (arrived,) = exchange(
        [(local_best.reshape(owner_count, query_count, -1), "clus", False)], AXES, sizes, 3
    )
    probe_owner = probe_places // owned_count
    earlier = jnp.arange(probe_count)[:, None] > jnp.arange(probe_count)[None, :]
    repeated = jnp.any(
        (probe_owner[:, :, None] == probe_owner[:, None, :]) & earlier[None], axis=2
    )
    owner_ids = jnp.arange(owner_count, dtype=jnp.int32)
    pick = probe_owner[:, :, None] == owner_ids[None, None, :]
    lists = jnp.transpose(arrived, (1, 0, 2))
    chosen = jnp.max(jnp.where(pick[..., None], lists[:, None], -jnp.inf), axis=2)
    chosen = jnp.where(repeated[..., None], masked_score, chosen)
    narrowed = lax.top_k(chosen.reshape(query_count, -1), TOPK)[0]
    (gathered,) = exchange([(narrowed, "feat", True)], AXES, sizes, 4)
    gathered = jnp.transpose(gathered, (1, 0, 2)).reshape(query_count, -1)
    return lax.top_k(gathered, TOPK)[0]


def solution(mesh):
    return jax.shard_map(
        body,
        mesh=mesh,
        in_specs=(
            P("clus", "feat"),
            P(None, "feat"),
            P("feat"),
            P("feat", None),
            P("clus"),
            P(),
            P("clus", "feat", None),
            P("clus"),
            P("clus", None),
            P("clus", None),
        ),
        out_specs=P("clus", None),
        check_vma=False,
    )
```

```python
import jax
import jax.numpy as jnp
from jax import lax
from jax.experimental import pallas as pl
from jax.experimental.pallas import tpu as pltpu
from jax.sharding import PartitionSpec as P

TOPK = 128


masked_score = -1e30
unit_scale = 0.0625
AXES = ("feat", "clus")

MESH = pl.DeviceIdType.MESH


def exchange(jobs, axes, sizes, collective_id):
    count = len(jobs)
    widest = max(sizes[axis] for _, axis, _ in jobs)
    used_axes = sorted({axis for _, axis, _ in jobs}, key=axes.index)
    shapes = []
    for x, axis, spread in jobs:
        shape = ((sizes[axis],) + x.shape) if spread else x.shape
        shapes.append(jax.ShapeDtypeStruct(shape, x.dtype))

    def kernel(*refs):
        ins, outs = refs[:count], refs[count : 2 * count]
        send_sem, recv_sem, own_sem = refs[2 * count :]
        where = {a: lax.axis_index(a) for a in axes}

        def device(axis, peer):
            return tuple(peer if a == axis else where[a] for a in axes)

        barrier = pltpu.get_barrier_semaphore()
        peers = 0
        for axis in used_axes:
            n = sizes[axis]
            for step in range(1, n):
                pl.semaphore_signal(
                    barrier,
                    inc=1,
                    device_id=device(axis, lax.rem(where[axis] + step, n)),
                    device_id_type=MESH,
                )
            peers += n - 1
        pl.semaphore_wait(barrier, peers)
        started = []
        locals_ = []
        for job, (x, axis, spread) in enumerate(jobs):
            n = sizes[axis]
            me = where[axis]
            src_of = (lambda d, job=job: ins[job]) if spread else (lambda d, job=job: ins[job].at[d])
            own = pltpu.make_async_copy(src_of(me), outs[job].at[me], own_sem.at[job])
            own.start()
            locals_.append(own)
            for step in range(1, n):
                peer = lax.rem(me + step, n)
                copy = pltpu.make_async_remote_copy(
                    src_ref=src_of(peer),
                    dst_ref=outs[job].at[me],
                    send_sem=send_sem.at[job, step],
                    recv_sem=recv_sem.at[job, step],
                    device_id=device(axis, peer),
                    device_id_type=MESH,
                )
                copy.start()
                started.append(copy)
        for copy in started:
            copy.wait_send()
        for copy in locals_:
            copy.wait()
        for job, (x, axis, spread) in enumerate(jobs):
            n = sizes[axis]
            me = where[axis]
            src_of = (lambda d, job=job: ins[job]) if spread else (lambda d, job=job: ins[job].at[d])
            for step in range(1, n):
                source = lax.rem(me + n - step, n)
                pltpu.make_async_copy(
                    src_of(source), outs[job].at[source], recv_sem.at[job, step]
                ).wait()

    return pl.pallas_call(
        kernel,
        out_shape=tuple(shapes),
        in_specs=[pl.BlockSpec(memory_space=pl.ANY)] * count,
        out_specs=tuple(pl.BlockSpec(memory_space=pl.ANY) for _ in jobs),
        scratch_shapes=[
            pltpu.SemaphoreType.DMA((count, widest)),
            pltpu.SemaphoreType.DMA((count, widest)),
            pltpu.SemaphoreType.DMA((count,)),
        ],
        compiler_params=pltpu.CompilerParams(collective_id=collective_id, has_side_effects=True),
    )(*[x for x, _, _ in jobs])


def compare_split(x, k, j):
    n = x.shape[0]
    tile = x.shape[1:]
    if k == 0:
        v = x.reshape((n // (2 * j), 2, j) + tile)
        a, b = v[:, 0], v[:, 1]
        return jnp.stack([jnp.maximum(a, b), jnp.minimum(a, b)], axis=1).reshape(x.shape)
    v = x.reshape((n // (2 * k), 2, k // (2 * j), 2, j) + tile)
    up_a, up_b = v[:, 0, :, 0], v[:, 0, :, 1]
    down_a, down_b = v[:, 1, :, 0], v[:, 1, :, 1]
    up = jnp.stack([jnp.minimum(up_a, up_b), jnp.maximum(up_a, up_b)], axis=2)
    down = jnp.stack([jnp.maximum(down_a, down_b), jnp.minimum(down_a, down_b)], axis=2)
    return jnp.stack([up, down], axis=1).reshape(x.shape)


def top_half_kernel(x_ref, o_ref, held):
    x = x_ref[...]
    n = x.shape[0]
    half = n // 2
    k = 2
    while k <= half:
        j = k // 2
        while j >= 1:
            x = compare_split(x, k, j)
            j //= 2
        k *= 2
    x = jnp.maximum(x[:half], x[half:])
    j = half // 2
    while j >= 1:
        x = compare_split(x, 0, j)
        j //= 2
    held[...] = x
    lanes = x.shape[2]
    for row in range(x.shape[1]):
        o_ref[pl.ds(row * lanes, lanes), :] = jnp.transpose(held[:, row, :])


def top_half(x):
    n = x.shape[0]
    return pl.pallas_call(
        top_half_kernel,
        out_shape=jax.ShapeDtypeStruct((x.shape[1] * x.shape[2], n // 2), x.dtype),
        in_specs=[pl.BlockSpec(memory_space=pltpu.VMEM)],
        out_specs=pl.BlockSpec(memory_space=pltpu.VMEM),
        scratch_shapes=[pltpu.VMEM((n // 2,) + x.shape[1:], x.dtype)],
    )(x)


def one_hot_take(table, index):
    ids = jnp.arange(table.shape[0], dtype=jnp.int32)
    hit = index[..., None] == ids
    return jnp.sum(jnp.where(hit, table, 0), axis=-1)


def body(
    item_feats,
    w_hidden,
    b_hidden,
    w_out,
    item_cluster,
    cluster_slot,
    catalog,
    cluster_fill,
    queries,
    probes,
):
    feat_count = lax.axis_size("feat")
    owner_count = lax.axis_size("clus")
    sizes = {"feat": feat_count, "clus": owner_count}
    feat_index = lax.axis_index("feat")
    owner_index = lax.axis_index("clus")
    device_rows = item_feats.shape[0] // feat_count
    emb_width = queries.shape[1]
    owned_count, row_dev = catalog.shape[:2]
    query_count = queries.shape[0]
    probe_count = probes.shape[1]

    probe_places = one_hot_take(cluster_slot, probes)
    probe_row = probe_places.reshape(-1, emb_width).astype(jnp.bfloat16)
    probe_lines = probe_row.shape[0]
    asked = jnp.concatenate([queries, probe_row], axis=0)
    lanes = 128
    asks, feats_all = exchange(
        [(asked, "clus", True), (item_feats.reshape(-1, lanes), "feat", True)], AXES, sizes, 0
    )

    feats_all = feats_all.reshape((feat_count,) + item_feats.shape)
    feats = jnp.transpose(feats_all, (1, 0, 2)).reshape(feats_all.shape[1], -1)
    pre_act = jnp.dot(feats, w_hidden, preferred_element_type=jnp.float32)
    hidden = jax.nn.silu(pre_act + b_hidden.astype(jnp.float32)).astype(jnp.bfloat16)
    partial = jnp.dot(hidden, w_out, preferred_element_type=jnp.float32)
    (parts,) = exchange(
        [(partial.reshape(feat_count, device_rows, -1), "feat", False)], AXES, sizes, 1
    )
    projected = jnp.sum(parts, axis=0)
    scaling = lax.rsqrt(jnp.mean(projected * projected, axis=1, keepdims=True) + 1e-06) * unit_scale
    embedded = (projected * scaling).astype(jnp.bfloat16)

    my_clusters = lax.dynamic_slice_in_dim(item_cluster, feat_index * device_rows, device_rows, 0)
    my_places = one_hot_take(cluster_slot, my_clusters)
    target = my_places // owned_count
    capacity = 2 * device_rows // owner_count
    owner_hot = (target[:, None] == jnp.arange(owner_count, dtype=jnp.int32)[None, :]).astype(
        jnp.int32
    )
    before = jnp.cumsum(owner_hot, axis=0) - owner_hot
    position = jnp.sum(before * owner_hot, axis=1)
    send_slot = target * capacity + position
    slots = owner_count * capacity
    slot_hot = send_slot[None, :] == jnp.arange(slots, dtype=jnp.int32)[:, None]
    send_rows = jnp.dot(
        slot_hot.astype(jnp.bfloat16), embedded, preferred_element_type=jnp.float32
    ).astype(jnp.bfloat16)
    send_places = jnp.sum(jnp.where(slot_hot, my_places[None, :] + 1, 0), axis=1) - 1
    place_row = jnp.full((owner_count, emb_width), -1, jnp.int32)
    place_row = place_row.at[:, :capacity].set(send_places.reshape(owner_count, capacity))
    lines = (capacity + 1 + 7) // 8 * 8
    routed = jnp.concatenate(
        [
            send_rows.reshape(owner_count, capacity, emb_width),
            place_row.astype(jnp.bfloat16)[:, None, :],
            jnp.zeros((owner_count, lines - capacity - 1, emb_width), jnp.bfloat16),
        ],
        axis=1,
    )
    (got,) = exchange([(routed, "clus", False)], AXES, sizes, 2)
    got_rows = got[:, :capacity].reshape(-1, emb_width)
    got_places = got[:, capacity, :capacity].astype(jnp.int32).reshape(-1)
    all_queries = asks[:, :query_count].reshape(-1, emb_width)
    all_probes = (
        asks[:, query_count : query_count + probe_lines]
        .astype(jnp.int32)
        .reshape(owner_count * query_count, probe_count)
    )

    first_owned = owner_index * owned_count
    local_ids = jnp.arange(owned_count, dtype=jnp.int32)
    owned_ids = first_owned + local_ids
    row_number = feat_index * row_dev + jnp.arange(row_dev, dtype=jnp.int32)
    stored_live = row_number[None, :] < cluster_fill[:, None]
    probed = jnp.any(all_probes[:, :, None] == owned_ids[None, None, :], axis=1)
    stored_allowed = (jnp.transpose(probed)[:, None, :] & stored_live[:, :, None]).reshape(
        owned_count * row_dev, -1
    )
    fresh_allowed = jnp.any(
        got_places[:, None, None] == jnp.transpose(all_probes)[None, :, :], axis=1
    )
    allowed = jnp.concatenate([stored_allowed, fresh_allowed], axis=0)
    scored_rows = jnp.concatenate(
        [catalog.reshape(owned_count * row_dev, emb_width), got_rows], 0
    )
    lanes = 128
    tiled_queries = all_queries.reshape(-1, lanes, emb_width)
    scores = jnp.einsum(
        "rd,sld->rsl", scored_rows, tiled_queries, preferred_element_type=jnp.float32
    )
    scores = jnp.where(allowed.reshape(scores.shape), scores, masked_score)
    local_best = top_half(scores)

    (arrived,) = exchange(
        [(local_best.reshape(owner_count, query_count, -1), "clus", False)], AXES, sizes, 3
    )
    probe_owner = probe_places // owned_count
    earlier = jnp.arange(probe_count)[:, None] > jnp.arange(probe_count)[None, :]
    repeated = jnp.any(
        (probe_owner[:, :, None] == probe_owner[:, None, :]) & earlier[None], axis=2
    )
    owner_ids = jnp.arange(owner_count, dtype=jnp.int32)
    pick = probe_owner[:, :, None] == owner_ids[None, None, :]
    pick = jnp.transpose(pick, (2, 0, 1))
    chosen = jnp.max(jnp.where(pick[..., None], arrived[:, :, None, :], -jnp.inf), axis=0)
    chosen = jnp.where(repeated[..., None], masked_score, chosen)
    narrowed = lax.top_k(chosen.reshape(query_count, -1), TOPK)[0]
    (gathered,) = exchange([(narrowed, "feat", True)], AXES, sizes, 4)
    gathered = jnp.transpose(gathered, (1, 0, 2)).reshape(query_count, -1)
    return lax.top_k(gathered, TOPK)[0]


def solution(mesh):
    return jax.shard_map(
        body,
        mesh=mesh,
        in_specs=(
            P("clus", "feat"),
            P(None, "feat"),
            P("feat"),
            P("feat", None),
            P("clus"),
            P(),
            P("clus", "feat", None),
            P("clus"),
            P("clus", None),
            P("clus", None),
        ),
        out_specs=P("clus", None),
        check_vma=False,
    )
```

```python
import jax
import jax.numpy as jnp
from jax import lax
from jax.experimental import pallas as pl
from jax.experimental.pallas import tpu as pltpu
from jax.sharding import PartitionSpec as P

TOPK = 128


masked_score = -1e30
unit_scale = 0.0625
AXES = ("feat", "clus")

MESH = pl.DeviceIdType.MESH


def exchange(jobs, axes, sizes, collective_id):
    count = len(jobs)
    widest = max(sizes[axis] for _, axis, _ in jobs)
    used_axes = sorted({axis for _, axis, _ in jobs}, key=axes.index)
    shapes = []
    for x, axis, spread in jobs:
        shape = ((sizes[axis],) + x.shape) if spread else x.shape
        shapes.append(jax.ShapeDtypeStruct(shape, x.dtype))

    def kernel(*refs):
        ins, outs = refs[:count], refs[count : 2 * count]
        send_sem, recv_sem, own_sem = refs[2 * count :]
        where = {a: lax.axis_index(a) for a in axes}

        def device(axis, peer):
            return tuple(peer if a == axis else where[a] for a in axes)

        barrier = pltpu.get_barrier_semaphore()
        peers = 0
        for axis in used_axes:
            n = sizes[axis]
            for step in range(1, n):
                pl.semaphore_signal(
                    barrier,
                    inc=1,
                    device_id=device(axis, lax.rem(where[axis] + step, n)),
                    device_id_type=MESH,
                )
            peers += n - 1
        pl.semaphore_wait(barrier, peers)
        started = []
        locals_ = []
        for job, (x, axis, spread) in enumerate(jobs):
            n = sizes[axis]
            me = where[axis]
            src_of = (lambda d, job=job: ins[job]) if spread else (lambda d, job=job: ins[job].at[d])
            own = pltpu.make_async_copy(src_of(me), outs[job].at[me], own_sem.at[job])
            own.start()
            locals_.append(own)
            for step in range(1, n):
                peer = lax.rem(me + step, n)
                copy = pltpu.make_async_remote_copy(
                    src_ref=src_of(peer),
                    dst_ref=outs[job].at[me],
                    send_sem=send_sem.at[job, step],
                    recv_sem=recv_sem.at[job, step],
                    device_id=device(axis, peer),
                    device_id_type=MESH,
                )
                copy.start()
                started.append(copy)
        for copy in started:
            copy.wait_send()
        for copy in locals_:
            copy.wait()
        for job, (x, axis, spread) in enumerate(jobs):
            n = sizes[axis]
            me = where[axis]
            src_of = (lambda d, job=job: ins[job]) if spread else (lambda d, job=job: ins[job].at[d])
            for step in range(1, n):
                source = lax.rem(me + n - step, n)
                pltpu.make_async_copy(
                    src_of(source), outs[job].at[source], recv_sem.at[job, step]
                ).wait()

    return pl.pallas_call(
        kernel,
        out_shape=tuple(shapes),
        in_specs=[pl.BlockSpec(memory_space=pl.ANY)] * count,
        out_specs=tuple(pl.BlockSpec(memory_space=pl.ANY) for _ in jobs),
        scratch_shapes=[
            pltpu.SemaphoreType.DMA((count, widest)),
            pltpu.SemaphoreType.DMA((count, widest)),
            pltpu.SemaphoreType.DMA((count,)),
        ],
        compiler_params=pltpu.CompilerParams(collective_id=collective_id, has_side_effects=True),
    )(*[x for x, _, _ in jobs])


def compare_split(x, k, j):
    n = x.shape[0]
    tile = x.shape[1:]
    if k == 0:
        v = x.reshape((n // (2 * j), 2, j) + tile)
        a, b = v[:, 0], v[:, 1]
        return jnp.stack([jnp.maximum(a, b), jnp.minimum(a, b)], axis=1).reshape(x.shape)
    v = x.reshape((n // (2 * k), 2, k // (2 * j), 2, j) + tile)
    up_a, up_b = v[:, 0, :, 0], v[:, 0, :, 1]
    down_a, down_b = v[:, 1, :, 0], v[:, 1, :, 1]
    up = jnp.stack([jnp.minimum(up_a, up_b), jnp.maximum(up_a, up_b)], axis=2)
    down = jnp.stack([jnp.maximum(down_a, down_b), jnp.minimum(down_a, down_b)], axis=2)
    return jnp.stack([up, down], axis=1).reshape(x.shape)


def top_half_kernel(x_ref, o_ref, held):
    x = x_ref[...]
    n = x.shape[0]
    half = n // 2
    k = 2
    while k <= half:
        j = k // 2
        while j >= 1:
            x = compare_split(x, k, j)
            j //= 2
        k *= 2
    x = jnp.maximum(x[:half], x[half:])
    j = half // 2
    while j >= 1:
        x = compare_split(x, 0, j)
        j //= 2
    held[...] = x
    lanes = x.shape[2]
    for row in range(x.shape[1]):
        o_ref[pl.ds(row * lanes, lanes), :] = jnp.transpose(held[:, row, :])


def top_half(x):
    n = x.shape[0]
    return pl.pallas_call(
        top_half_kernel,
        out_shape=jax.ShapeDtypeStruct((x.shape[1] * x.shape[2], n // 2), x.dtype),
        in_specs=[pl.BlockSpec(memory_space=pltpu.VMEM)],
        out_specs=pl.BlockSpec(memory_space=pltpu.VMEM),
        scratch_shapes=[pltpu.VMEM((n // 2,) + x.shape[1:], x.dtype)],
    )(x)


def one_hot_take(table, index):
    ids = jnp.arange(table.shape[0], dtype=jnp.int32)
    hit = index[..., None] == ids
    return jnp.sum(jnp.where(hit, table, 0), axis=-1)


def body(
    item_feats,
    w_hidden,
    b_hidden,
    w_out,
    item_cluster,
    cluster_slot,
    catalog,
    cluster_fill,
    queries,
    probes,
):
    feat_count = lax.axis_size("feat")
    owner_count = lax.axis_size("clus")
    sizes = {"feat": feat_count, "clus": owner_count}
    feat_index = lax.axis_index("feat")
    owner_index = lax.axis_index("clus")
    device_rows = item_feats.shape[0] // feat_count
    emb_width = queries.shape[1]
    owned_count, row_dev = catalog.shape[:2]
    query_count = queries.shape[0]
    probe_count = probes.shape[1]

    probe_places = one_hot_take(cluster_slot, probes)
    probe_row = probe_places.reshape(-1, emb_width).astype(jnp.bfloat16)
    probe_lines = probe_row.shape[0]
    asked = jnp.concatenate([queries, probe_row], axis=0)
    lanes = 128
    asks, feats_all = exchange(
        [(asked, "clus", True), (item_feats.reshape(-1, lanes), "feat", True)], AXES, sizes, 0
    )

    feats_all = feats_all.reshape((feat_count,) + item_feats.shape)
    feats = jnp.transpose(feats_all, (1, 0, 2)).reshape(feats_all.shape[1], -1)
    pre_act = jnp.dot(feats, w_hidden, preferred_element_type=jnp.float32)
    hidden = jax.nn.silu(pre_act + b_hidden.astype(jnp.float32)).astype(jnp.bfloat16)
    partial = jnp.dot(hidden, w_out, preferred_element_type=jnp.float32)
    (parts,) = exchange(
        [(partial.reshape(feat_count, device_rows, -1), "feat", False)], AXES, sizes, 1
    )
    projected = jnp.sum(parts, axis=0)
    scaling = lax.rsqrt(jnp.mean(projected * projected, axis=1, keepdims=True) + 1e-06) * unit_scale
    embedded = (projected * scaling).astype(jnp.bfloat16)

    my_clusters = lax.dynamic_slice_in_dim(item_cluster, feat_index * device_rows, device_rows, 0)
    my_places = one_hot_take(cluster_slot, my_clusters)
    all_queries = asks[:, :query_count].reshape(-1, emb_width)
    all_probes = (
        asks[:, query_count : query_count + probe_lines]
        .astype(jnp.int32)
        .reshape(owner_count * query_count, probe_count)
    )

    first_owned = owner_index * owned_count
    local_ids = jnp.arange(owned_count, dtype=jnp.int32)
    owned_ids = first_owned + local_ids
    row_number = feat_index * row_dev + jnp.arange(row_dev, dtype=jnp.int32)
    stored_live = row_number[None, :] < cluster_fill[:, None]
    probed = jnp.any(all_probes[:, :, None] == owned_ids[None, None, :], axis=1)
    stored_allowed = (jnp.transpose(probed)[:, None, :] & stored_live[:, :, None]).reshape(
        owned_count * row_dev, -1
    )
    fresh_allowed = jnp.any(
        my_places[:, None, None] == jnp.transpose(all_probes)[None, :, :], axis=1
    )
    pad_rows = 2 * TOPK - owned_count * row_dev - device_rows
    allowed = jnp.concatenate(
        [stored_allowed, fresh_allowed, jnp.zeros((pad_rows, stored_allowed.shape[1]), bool)],
        axis=0,
    )
    scored_rows = jnp.concatenate(
        [
            catalog.reshape(owned_count * row_dev, emb_width),
            embedded,
            jnp.zeros((pad_rows, emb_width), embedded.dtype),
        ],
        0,
    )
    lanes = 128
    tiled_queries = all_queries.reshape(-1, lanes, emb_width)
    scores = jnp.einsum(
        "rd,sld->rsl", scored_rows, tiled_queries, preferred_element_type=jnp.float32
    )
    scores = jnp.where(allowed.reshape(scores.shape), scores, masked_score)
    local_best = top_half(scores)

    (arrived,) = exchange(
        [(local_best.reshape(owner_count, query_count, -1), "clus", False)], AXES, sizes, 3
    )
    lists = jnp.transpose(arrived, (1, 0, 2)).reshape(query_count, -1)
    narrowed = lax.top_k(lists, TOPK)[0]
    (gathered,) = exchange([(narrowed, "feat", True)], AXES, sizes, 4)
    gathered = jnp.transpose(gathered, (1, 0, 2)).reshape(query_count, -1)
    return lax.top_k(gathered, TOPK)[0]


def solution(mesh):
    return jax.shard_map(
        body,
        mesh=mesh,
        in_specs=(
            P("clus", "feat"),
            P(None, "feat"),
            P("feat"),
            P("feat", None),
            P("clus"),
            P(),
            P("clus", "feat", None),
            P("clus"),
            P("clus", None),
            P("clus", None),
        ),
        out_specs=P("clus", None),
        check_vma=False,
    )
```

```python
import jax
import jax.numpy as jnp
from jax import lax
from jax.experimental import pallas as pl
from jax.experimental.pallas import tpu as pltpu
from jax.sharding import PartitionSpec as P

TOPK = 128


masked_score = -1e30
unit_scale = 0.0625
AXES = ("feat", "clus")

MESH = pl.DeviceIdType.MESH


def exchange(jobs, axes, sizes, collective_id):
    count = len(jobs)
    widest = max(sizes[axis] for _, axis, _ in jobs)
    used_axes = sorted({axis for _, axis, _ in jobs}, key=axes.index)
    shapes = []
    for x, axis, spread in jobs:
        shape = ((sizes[axis],) + x.shape) if spread else x.shape
        shapes.append(jax.ShapeDtypeStruct(shape, x.dtype))

    def kernel(*refs):
        ins, outs = refs[:count], refs[count : 2 * count]
        send_sem, recv_sem, own_sem = refs[2 * count :]
        where = {a: lax.axis_index(a) for a in axes}

        def device(axis, peer):
            return tuple(peer if a == axis else where[a] for a in axes)

        barrier = pltpu.get_barrier_semaphore()
        peers = 0
        for axis in used_axes:
            n = sizes[axis]
            for step in range(1, n):
                pl.semaphore_signal(
                    barrier,
                    inc=1,
                    device_id=device(axis, lax.rem(where[axis] + step, n)),
                    device_id_type=MESH,
                )
            peers += n - 1
        pl.semaphore_wait(barrier, peers)
        started = []
        locals_ = []
        for job, (x, axis, spread) in enumerate(jobs):
            n = sizes[axis]
            me = where[axis]
            src_of = (lambda d, job=job: ins[job]) if spread else (lambda d, job=job: ins[job].at[d])
            own = pltpu.make_async_copy(src_of(me), outs[job].at[me], own_sem.at[job])
            own.start()
            locals_.append(own)
            for step in range(1, n):
                peer = lax.rem(me + step, n)
                copy = pltpu.make_async_remote_copy(
                    src_ref=src_of(peer),
                    dst_ref=outs[job].at[me],
                    send_sem=send_sem.at[job, step],
                    recv_sem=recv_sem.at[job, step],
                    device_id=device(axis, peer),
                    device_id_type=MESH,
                )
                copy.start()
                started.append(copy)
        for copy in started:
            copy.wait_send()
        for copy in locals_:
            copy.wait()
        for job, (x, axis, spread) in enumerate(jobs):
            n = sizes[axis]
            me = where[axis]
            src_of = (lambda d, job=job: ins[job]) if spread else (lambda d, job=job: ins[job].at[d])
            for step in range(1, n):
                source = lax.rem(me + n - step, n)
                pltpu.make_async_copy(
                    src_of(source), outs[job].at[source], recv_sem.at[job, step]
                ).wait()

    return pl.pallas_call(
        kernel,
        out_shape=tuple(shapes),
        in_specs=[pl.BlockSpec(memory_space=pl.ANY)] * count,
        out_specs=tuple(pl.BlockSpec(memory_space=pl.ANY) for _ in jobs),
        scratch_shapes=[
            pltpu.SemaphoreType.DMA((count, widest)),
            pltpu.SemaphoreType.DMA((count, widest)),
            pltpu.SemaphoreType.DMA((count,)),
        ],
        compiler_params=pltpu.CompilerParams(collective_id=collective_id, has_side_effects=True),
    )(*[x for x, _, _ in jobs])


def compare_split(x, k, j):
    n = x.shape[0]
    tile = x.shape[1:]
    if k == 0:
        v = x.reshape((n // (2 * j), 2, j) + tile)
        a, b = v[:, 0], v[:, 1]
        return jnp.stack([jnp.maximum(a, b), jnp.minimum(a, b)], axis=1).reshape(x.shape)
    v = x.reshape((n // (2 * k), 2, k // (2 * j), 2, j) + tile)
    up_a, up_b = v[:, 0, :, 0], v[:, 0, :, 1]
    down_a, down_b = v[:, 1, :, 0], v[:, 1, :, 1]
    up = jnp.stack([jnp.minimum(up_a, up_b), jnp.maximum(up_a, up_b)], axis=2)
    down = jnp.stack([jnp.maximum(down_a, down_b), jnp.minimum(down_a, down_b)], axis=2)
    return jnp.stack([up, down], axis=1).reshape(x.shape)


def top_half_kernel(x_ref, o_ref, held):
    x = x_ref[...]
    n = x.shape[0]
    half = n // 2
    k = 2
    while k <= half:
        j = k // 2
        while j >= 1:
            x = compare_split(x, k, j)
            j //= 2
        k *= 2
    x = jnp.maximum(x[:half], x[half:])
    j = half // 2
    while j >= 1:
        x = compare_split(x, 0, j)
        j //= 2
    held[...] = x
    lanes = x.shape[2]
    for row in range(x.shape[1]):
        o_ref[pl.ds(row * lanes, lanes), :] = jnp.transpose(held[:, row, :])


def top_half(x):
    n = x.shape[0]
    return pl.pallas_call(
        top_half_kernel,
        out_shape=jax.ShapeDtypeStruct((x.shape[1] * x.shape[2], n // 2), x.dtype),
        in_specs=[pl.BlockSpec(memory_space=pltpu.VMEM)],
        out_specs=pl.BlockSpec(memory_space=pltpu.VMEM),
        scratch_shapes=[pltpu.VMEM((n // 2,) + x.shape[1:], x.dtype)],
    )(x)


def merge_kernel(steps, x_ref, o_ref, held):
    x = x_ref[...]
    n = x.shape[0]
    for axis, shift in steps:
        partner = pltpu.roll(x, shift, axis)
        flipped = jnp.stack([partner[n - 1 - r] for r in range(n)], axis=0)
        x = jnp.maximum(x, flipped)
        j = n // 2
        while j >= 1:
            x = compare_split(x, 0, j)
            j //= 2
    held[...] = x
    o_ref[...] = held[:, 0, :]


def merge_lists(x, steps):
    return pl.pallas_call(
        lambda *refs: merge_kernel(steps, *refs),
        out_shape=jax.ShapeDtypeStruct((x.shape[0], x.shape[2]), x.dtype),
        in_specs=[pl.BlockSpec(memory_space=pltpu.VMEM)],
        out_specs=pl.BlockSpec(memory_space=pltpu.VMEM),
        scratch_shapes=[pltpu.VMEM(x.shape, x.dtype)],
    )(x)


def one_hot_take(table, index):
    ids = jnp.arange(table.shape[0], dtype=jnp.int32)
    hit = index[..., None] == ids
    return jnp.sum(jnp.where(hit, table, 0), axis=-1)


def body(
    item_feats,
    w_hidden,
    b_hidden,
    w_out,
    item_cluster,
    cluster_slot,
    catalog,
    cluster_fill,
    queries,
    probes,
):
    feat_count = lax.axis_size("feat")
    owner_count = lax.axis_size("clus")
    sizes = {"feat": feat_count, "clus": owner_count}
    feat_index = lax.axis_index("feat")
    owner_index = lax.axis_index("clus")
    device_rows = item_feats.shape[0] // feat_count
    emb_width = queries.shape[1]
    owned_count, row_dev = catalog.shape[:2]
    query_count = queries.shape[0]
    probe_count = probes.shape[1]

    probe_places = one_hot_take(cluster_slot, probes)
    probe_row = probe_places.reshape(-1, emb_width).astype(jnp.bfloat16)
    probe_lines = probe_row.shape[0]
    asked = jnp.concatenate([queries, probe_row], axis=0)
    lanes = 128
    asks, feats_all = exchange(
        [(asked, "clus", True), (item_feats.reshape(-1, lanes), "feat", True)], AXES, sizes, 0
    )

    feats_all = feats_all.reshape((feat_count,) + item_feats.shape)
    feats = jnp.transpose(feats_all, (1, 0, 2)).reshape(feats_all.shape[1], -1)
    pre_act = jnp.dot(feats, w_hidden, preferred_element_type=jnp.float32)
    hidden = jax.nn.silu(pre_act + b_hidden.astype(jnp.float32)).astype(jnp.bfloat16)
    partial = jnp.dot(hidden, w_out, preferred_element_type=jnp.float32)
    (parts,) = exchange(
        [(partial.reshape(feat_count, device_rows, -1), "feat", False)], AXES, sizes, 1
    )
    projected = jnp.sum(parts, axis=0)
    scaling = lax.rsqrt(jnp.mean(projected * projected, axis=1, keepdims=True) + 1e-06) * unit_scale
    embedded = (projected * scaling).astype(jnp.bfloat16)

    my_clusters = lax.dynamic_slice_in_dim(item_cluster, feat_index * device_rows, device_rows, 0)
    my_places = one_hot_take(cluster_slot, my_clusters)
    all_queries = asks[:, :query_count].reshape(-1, emb_width)
    all_probes = (
        asks[:, query_count : query_count + probe_lines]
        .astype(jnp.int32)
        .reshape(owner_count * query_count, probe_count)
    )

    first_owned = owner_index * owned_count
    local_ids = jnp.arange(owned_count, dtype=jnp.int32)
    owned_ids = first_owned + local_ids
    row_number = feat_index * row_dev + jnp.arange(row_dev, dtype=jnp.int32)
    stored_live = row_number[None, :] < cluster_fill[:, None]
    probed = jnp.any(all_probes[:, :, None] == owned_ids[None, None, :], axis=1)
    stored_allowed = (jnp.transpose(probed)[:, None, :] & stored_live[:, :, None]).reshape(
        owned_count * row_dev, -1
    )
    fresh_allowed = jnp.any(
        my_places[:, None, None] == jnp.transpose(all_probes)[None, :, :], axis=1
    )
    pad_rows = 2 * TOPK - owned_count * row_dev - device_rows
    allowed = jnp.concatenate(
        [stored_allowed, fresh_allowed, jnp.zeros((pad_rows, stored_allowed.shape[1]), bool)],
        axis=0,
    )
    scored_rows = jnp.concatenate(
        [
            catalog.reshape(owned_count * row_dev, emb_width),
            embedded,
            jnp.zeros((pad_rows, emb_width), embedded.dtype),
        ],
        0,
    )
    lanes = 128
    tiled_queries = all_queries.reshape(-1, lanes, emb_width)
    scores = jnp.einsum(
        "rd,sld->rsl", scored_rows, tiled_queries, preferred_element_type=jnp.float32
    )
    scores = jnp.where(allowed.reshape(scores.shape), scores, masked_score)
    local_best = top_half(scores)

    (arrived,) = exchange(
        [(local_best.reshape(owner_count, query_count, -1), "clus", False)], AXES, sizes, 3
    )
    sublanes, lanes = 8, 128
    groups = lanes // query_count
    lists = arrived.reshape(sublanes, groups, query_count, -1)
    lists = jnp.transpose(lists, (3, 0, 1, 2)).reshape(-1, sublanes, lanes)
    steps = [(2, query_count * 2**i) for i in range(groups.bit_length() - 1)]
    steps += [(1, 2**i) for i in range(sublanes.bit_length() - 1)]
    merged = merge_lists(lists, tuple(steps))
    narrowed = jnp.transpose(merged[:, :query_count])
    (gathered,) = exchange([(narrowed, "feat", True)], AXES, sizes, 4)
    lists = jnp.tile(jnp.transpose(gathered, (2, 0, 1)), (1, 1, groups))
    steps = [(1, 2**i) for i in range(feat_count.bit_length() - 1)]
    merged = merge_lists(lists, tuple(steps))
    return jnp.transpose(merged[:, :query_count])


def solution(mesh):
    return jax.shard_map(
        body,
        mesh=mesh,
        in_specs=(
            P("clus", "feat"),
            P(None, "feat"),
            P("feat"),
            P("feat", None),
            P("clus"),
            P(),
            P("clus", "feat", None),
            P("clus"),
            P("clus", None),
            P("clus", None),
        ),
        out_specs=P("clus", None),
        check_vma=False,
    )
```

```python
import jax
import jax.numpy as jnp
from jax import lax
from jax.experimental import pallas as pl
from jax.experimental.pallas import tpu as pltpu
from jax.sharding import PartitionSpec as P

TOPK = 128


masked_score = -1e30
unit_scale = 0.0625
AXES = ("feat", "clus")

MESH = pl.DeviceIdType.MESH


def exchange(jobs, axes, sizes, collective_id):
    count = len(jobs)
    widest = max(sizes[axis] for _, axis, _ in jobs)
    used_axes = sorted({axis for _, axis, _ in jobs}, key=axes.index)
    shapes = []
    for x, axis, spread in jobs:
        shape = ((sizes[axis],) + x.shape) if spread else x.shape
        shapes.append(jax.ShapeDtypeStruct(shape, x.dtype))

    def kernel(*refs):
        ins, outs = refs[:count], refs[count : 2 * count]
        send_sem, recv_sem, own_sem = refs[2 * count :]
        where = {a: lax.axis_index(a) for a in axes}

        def device(axis, peer):
            return tuple(peer if a == axis else where[a] for a in axes)

        barrier = pltpu.get_barrier_semaphore()
        peers = 0
        for axis in used_axes:
            n = sizes[axis]
            for step in range(1, n):
                pl.semaphore_signal(
                    barrier,
                    inc=1,
                    device_id=device(axis, lax.rem(where[axis] + step, n)),
                    device_id_type=MESH,
                )
            peers += n - 1
        pl.semaphore_wait(barrier, peers)
        started = []
        locals_ = []
        for job, (x, axis, spread) in enumerate(jobs):
            n = sizes[axis]
            me = where[axis]
            src_of = (lambda d, job=job: ins[job]) if spread else (lambda d, job=job: ins[job].at[d])
            own = pltpu.make_async_copy(src_of(me), outs[job].at[me], own_sem.at[job])
            own.start()
            locals_.append(own)
            for step in range(1, n):
                peer = lax.rem(me + step, n)
                copy = pltpu.make_async_remote_copy(
                    src_ref=src_of(peer),
                    dst_ref=outs[job].at[me],
                    send_sem=send_sem.at[job, step],
                    recv_sem=recv_sem.at[job, step],
                    device_id=device(axis, peer),
                    device_id_type=MESH,
                )
                copy.start()
                started.append(copy)
        for copy in started:
            copy.wait_send()
        for copy in locals_:
            copy.wait()
        for job, (x, axis, spread) in enumerate(jobs):
            n = sizes[axis]
            me = where[axis]
            src_of = (lambda d, job=job: ins[job]) if spread else (lambda d, job=job: ins[job].at[d])
            for step in range(1, n):
                source = lax.rem(me + n - step, n)
                pltpu.make_async_copy(
                    src_of(source), outs[job].at[source], recv_sem.at[job, step]
                ).wait()

    return pl.pallas_call(
        kernel,
        out_shape=tuple(shapes),
        in_specs=[pl.BlockSpec(memory_space=pl.ANY)] * count,
        out_specs=tuple(pl.BlockSpec(memory_space=pl.ANY) for _ in jobs),
        scratch_shapes=[
            pltpu.SemaphoreType.DMA((count, widest)),
            pltpu.SemaphoreType.DMA((count, widest)),
            pltpu.SemaphoreType.DMA((count,)),
        ],
        compiler_params=pltpu.CompilerParams(collective_id=collective_id, has_side_effects=True),
    )(*[x for x, _, _ in jobs])


def compare_split(x, k, j):
    n = x.shape[0]
    tile = x.shape[1:]
    if k == 0:
        v = x.reshape((n // (2 * j), 2, j) + tile)
        a, b = v[:, 0], v[:, 1]
        return jnp.stack([jnp.maximum(a, b), jnp.minimum(a, b)], axis=1).reshape(x.shape)
    v = x.reshape((n // (2 * k), 2, k // (2 * j), 2, j) + tile)
    up_a, up_b = v[:, 0, :, 0], v[:, 0, :, 1]
    down_a, down_b = v[:, 1, :, 0], v[:, 1, :, 1]
    up = jnp.stack([jnp.minimum(up_a, up_b), jnp.maximum(up_a, up_b)], axis=2)
    down = jnp.stack([jnp.maximum(down_a, down_b), jnp.minimum(down_a, down_b)], axis=2)
    return jnp.stack([up, down], axis=1).reshape(x.shape)


def top_half_kernel(x_ref, o_ref, spread, held):
    lanes = o_ref.shape[1]
    sublanes = spread.shape[1]
    for row in range(sublanes):
        spread[:, row, :] = x_ref[:, pl.ds(row * lanes, lanes)]
    x = spread[...]
    n = x.shape[0]
    half = n // 2
    k = 2
    while k <= half:
        j = k // 2
        while j >= 1:
            x = compare_split(x, k, j)
            j //= 2
        k *= 2
    x = jnp.maximum(x[:half], x[half:])
    j = half // 2
    while j >= 1:
        x = compare_split(x, 0, j)
        j //= 2
    held[...] = x
    for row in range(sublanes):
        o_ref[pl.ds(row * lanes, lanes), :] = jnp.transpose(held[:, row, :])


def top_half(x):
    n, width = x.shape
    sublanes = 8
    lanes = width // sublanes
    return pl.pallas_call(
        top_half_kernel,
        out_shape=jax.ShapeDtypeStruct((width, n // 2), x.dtype),
        in_specs=[pl.BlockSpec(memory_space=pltpu.VMEM)],
        out_specs=pl.BlockSpec(memory_space=pltpu.VMEM),
        scratch_shapes=[
            pltpu.VMEM((n, sublanes, lanes), x.dtype),
            pltpu.VMEM((n // 2, sublanes, lanes), x.dtype),
        ],
    )(x)


def merge_kernel(steps, x_ref, o_ref, held):
    x = x_ref[...]
    n = x.shape[0]
    for axis, shift in steps:
        partner = pltpu.roll(x, shift, axis)
        flipped = jnp.stack([partner[n - 1 - r] for r in range(n)], axis=0)
        x = jnp.maximum(x, flipped)
        j = n // 2
        while j >= 1:
            x = compare_split(x, 0, j)
            j //= 2
    held[...] = x
    o_ref[...] = jnp.transpose(held[:, 0, :])[: o_ref.shape[0]]


def merge_lists(x, steps, width):
    return pl.pallas_call(
        lambda *refs: merge_kernel(steps, *refs),
        out_shape=jax.ShapeDtypeStruct((width, x.shape[0]), x.dtype),
        in_specs=[pl.BlockSpec(memory_space=pltpu.VMEM)],
        out_specs=pl.BlockSpec(memory_space=pltpu.VMEM),
        scratch_shapes=[pltpu.VMEM(x.shape, x.dtype)],
    )(x)


def one_hot_take(table, index):
    ids = jnp.arange(table.shape[0], dtype=jnp.int32)
    hit = index[..., None] == ids
    return jnp.sum(jnp.where(hit, table, 0), axis=-1)


def body(
    item_feats,
    w_hidden,
    b_hidden,
    w_out,
    item_cluster,
    cluster_slot,
    catalog,
    cluster_fill,
    queries,
    probes,
):
    feat_count = lax.axis_size("feat")
    owner_count = lax.axis_size("clus")
    sizes = {"feat": feat_count, "clus": owner_count}
    feat_index = lax.axis_index("feat")
    owner_index = lax.axis_index("clus")
    device_rows = item_feats.shape[0] // feat_count
    emb_width = queries.shape[1]
    owned_count, row_dev = catalog.shape[:2]
    query_count = queries.shape[0]
    probe_count = probes.shape[1]

    probe_places = one_hot_take(cluster_slot, probes)
    probe_row = probe_places.reshape(-1, emb_width).astype(jnp.bfloat16)
    probe_lines = probe_row.shape[0]
    asked = jnp.concatenate([queries, probe_row], axis=0)
    lanes = 128
    asks, feats_all = exchange(
        [(asked, "clus", True), (item_feats.reshape(-1, lanes), "feat", True)], AXES, sizes, 0
    )

    feats_all = feats_all.reshape((feat_count,) + item_feats.shape)
    feats = jnp.transpose(feats_all, (1, 0, 2)).reshape(feats_all.shape[1], -1)
    pre_act = jnp.dot(feats, w_hidden, preferred_element_type=jnp.float32)
    hidden = jax.nn.silu(pre_act + b_hidden.astype(jnp.float32)).astype(jnp.bfloat16)
    partial = jnp.dot(hidden, w_out, preferred_element_type=jnp.float32)
    (parts,) = exchange(
        [(partial.reshape(feat_count, device_rows, -1), "feat", False)], AXES, sizes, 1
    )
    projected = jnp.sum(parts, axis=0)
    scaling = lax.rsqrt(jnp.mean(projected * projected, axis=1, keepdims=True) + 1e-06) * unit_scale
    embedded = (projected * scaling).astype(jnp.bfloat16)

    my_clusters = lax.dynamic_slice_in_dim(item_cluster, feat_index * device_rows, device_rows, 0)
    my_places = one_hot_take(cluster_slot, my_clusters)
    all_queries = asks[:, :query_count].reshape(-1, emb_width)
    all_probes = (
        asks[:, query_count : query_count + probe_lines]
        .astype(jnp.int32)
        .reshape(owner_count * query_count, probe_count)
    )

    first_owned = owner_index * owned_count
    local_ids = jnp.arange(owned_count, dtype=jnp.int32)
    owned_ids = first_owned + local_ids
    row_number = feat_index * row_dev + jnp.arange(row_dev, dtype=jnp.int32)
    stored_live = row_number[None, :] < cluster_fill[:, None]
    probed = jnp.any(all_probes[:, :, None] == owned_ids[None, None, :], axis=1)
    stored_allowed = (jnp.transpose(probed)[:, None, :] & stored_live[:, :, None]).reshape(
        owned_count * row_dev, -1
    )
    fresh_allowed = jnp.any(
        my_places[:, None, None] == jnp.transpose(all_probes)[None, :, :], axis=1
    )
    pad_rows = 2 * TOPK - owned_count * row_dev - device_rows
    allowed = jnp.concatenate(
        [stored_allowed, fresh_allowed, jnp.zeros((pad_rows, stored_allowed.shape[1]), bool)],
        axis=0,
    )
    scored_rows = jnp.concatenate(
        [
            catalog.reshape(owned_count * row_dev, emb_width),
            embedded,
            jnp.zeros((pad_rows, emb_width), embedded.dtype),
        ],
        0,
    )
    scores = jnp.einsum("rd,bd->rb", scored_rows, all_queries, preferred_element_type=jnp.float32)
    scores = jnp.where(allowed, scores, masked_score)
    local_best = top_half(scores)

    (arrived,) = exchange(
        [(local_best.reshape(owner_count, query_count, -1), "clus", False)], AXES, sizes, 3
    )
    sublanes, lanes = 8, 128
    groups = lanes // query_count
    lists = arrived.reshape(sublanes, groups, query_count, -1)
    lists = jnp.transpose(lists, (3, 0, 1, 2)).reshape(-1, sublanes, lanes)
    steps = [(2, query_count * 2**i) for i in range(groups.bit_length() - 1)]
    steps += [(1, 2**i) for i in range(sublanes.bit_length() - 1)]
    narrowed = merge_lists(lists, tuple(steps), query_count)
    (gathered,) = exchange([(narrowed, "feat", True)], AXES, sizes, 4)
    lists = jnp.tile(jnp.transpose(gathered, (2, 0, 1)), (1, 1, groups))
    steps = [(1, 2**i) for i in range(feat_count.bit_length() - 1)]
    return merge_lists(lists, tuple(steps), query_count)


def solution(mesh):
    return jax.shard_map(
        body,
        mesh=mesh,
        in_specs=(
            P("clus", "feat"),
            P(None, "feat"),
            P("feat"),
            P("feat", None),
            P("clus"),
            P(),
            P("clus", "feat", None),
            P("clus"),
            P("clus", None),
            P("clus", None),
        ),
        out_specs=P("clus", None),
        check_vma=False,
    )
```

```python
import jax
import jax.numpy as jnp
from jax import lax
from jax.experimental import pallas as pl
from jax.experimental.pallas import tpu as pltpu
from jax.sharding import PartitionSpec as P

TOPK = 128


masked_score = -1e30
unit_scale = 0.0625
AXES = ("feat", "clus")

MESH = pl.DeviceIdType.MESH


def exchange(jobs, axes, sizes, collective_id):
    count = len(jobs)
    widest = max(sizes[axis] for _, axis, _ in jobs)
    used_axes = sorted({axis for _, axis, _ in jobs}, key=axes.index)
    shapes = []
    for x, axis, spread in jobs:
        shape = ((sizes[axis],) + x.shape) if spread else x.shape
        shapes.append(jax.ShapeDtypeStruct(shape, x.dtype))

    def kernel(*refs):
        ins, outs = refs[:count], refs[count : 2 * count]
        send_sem, recv_sem, own_sem = refs[2 * count :]
        where = {a: lax.axis_index(a) for a in axes}

        def device(axis, peer):
            return tuple(peer if a == axis else where[a] for a in axes)

        barrier = pltpu.get_barrier_semaphore()
        peers = 0
        for axis in used_axes:
            n = sizes[axis]
            for step in range(1, n):
                pl.semaphore_signal(
                    barrier,
                    inc=1,
                    device_id=device(axis, lax.rem(where[axis] + step, n)),
                    device_id_type=MESH,
                )
            peers += n - 1
        pl.semaphore_wait(barrier, peers)
        started = []
        locals_ = []
        for job, (x, axis, spread) in enumerate(jobs):
            n = sizes[axis]
            me = where[axis]
            src_of = (lambda d, job=job: ins[job]) if spread else (lambda d, job=job: ins[job].at[d])
            own = pltpu.make_async_copy(src_of(me), outs[job].at[me], own_sem.at[job])
            own.start()
            locals_.append(own)
            for step in range(1, n):
                peer = lax.rem(me + step, n)
                copy = pltpu.make_async_remote_copy(
                    src_ref=src_of(peer),
                    dst_ref=outs[job].at[me],
                    send_sem=send_sem.at[job, step],
                    recv_sem=recv_sem.at[job, step],
                    device_id=device(axis, peer),
                    device_id_type=MESH,
                )
                copy.start()
                started.append(copy)
        for copy in started:
            copy.wait_send()
        for copy in locals_:
            copy.wait()
        for job, (x, axis, spread) in enumerate(jobs):
            n = sizes[axis]
            me = where[axis]
            src_of = (lambda d, job=job: ins[job]) if spread else (lambda d, job=job: ins[job].at[d])
            for step in range(1, n):
                source = lax.rem(me + n - step, n)
                pltpu.make_async_copy(
                    src_of(source), outs[job].at[source], recv_sem.at[job, step]
                ).wait()

    return pl.pallas_call(
        kernel,
        out_shape=tuple(shapes),
        in_specs=[pl.BlockSpec(memory_space=pl.ANY)] * count,
        out_specs=tuple(pl.BlockSpec(memory_space=pl.ANY) for _ in jobs),
        scratch_shapes=[
            pltpu.SemaphoreType.DMA((count, widest)),
            pltpu.SemaphoreType.DMA((count, widest)),
            pltpu.SemaphoreType.DMA((count,)),
        ],
        compiler_params=pltpu.CompilerParams(collective_id=collective_id, has_side_effects=True),
    )(*[x for x, _, _ in jobs])


def compare_split(x, k, j):
    n = x.shape[0]
    tile = x.shape[1:]
    if k == 0:
        v = x.reshape((n // (2 * j), 2, j) + tile)
        a, b = v[:, 0], v[:, 1]
        return jnp.stack([jnp.maximum(a, b), jnp.minimum(a, b)], axis=1).reshape(x.shape)
    v = x.reshape((n // (2 * k), 2, k // (2 * j), 2, j) + tile)
    up_a, up_b = v[:, 0, :, 0], v[:, 0, :, 1]
    down_a, down_b = v[:, 1, :, 0], v[:, 1, :, 1]
    up = jnp.stack([jnp.minimum(up_a, up_b), jnp.maximum(up_a, up_b)], axis=2)
    down = jnp.stack([jnp.maximum(down_a, down_b), jnp.minimum(down_a, down_b)], axis=2)
    return jnp.stack([up, down], axis=1).reshape(x.shape)


def top_half_kernel(x_ref, o_ref, spread, held):
    lanes = o_ref.shape[1]
    sublanes = spread.shape[1]
    for row in range(sublanes):
        spread[:, row, :] = x_ref[:, pl.ds(row * lanes, lanes)]
    x = spread[...]
    n = x.shape[0]
    half = n // 2
    k = 2
    while k <= half:
        j = k // 2
        while j >= 1:
            x = compare_split(x, k, j)
            j //= 2
        k *= 2
    x = jnp.maximum(x[:half], x[half:])
    j = half // 2
    while j >= 1:
        x = compare_split(x, 0, j)
        j //= 2
    held[...] = x
    for row in range(sublanes):
        o_ref[pl.ds(row * lanes, lanes), :] = jnp.transpose(held[:, row, :])


def top_half(x):
    n, width = x.shape
    sublanes = 8
    lanes = width // sublanes
    return pl.pallas_call(
        top_half_kernel,
        out_shape=jax.ShapeDtypeStruct((width, n // 2), x.dtype),
        in_specs=[pl.BlockSpec(memory_space=pltpu.VMEM)],
        out_specs=pl.BlockSpec(memory_space=pltpu.VMEM),
        scratch_shapes=[
            pltpu.VMEM((n, sublanes, lanes), x.dtype),
            pltpu.VMEM((n // 2, sublanes, lanes), x.dtype),
        ],
    )(x)


def merge_kernel(steps, x_ref, o_ref, held):
    sublanes, lanes = held.shape[1], held.shape[2]
    group = x_ref.shape[0] // sublanes
    for row in range(sublanes):
        block = x_ref[pl.ds(row * group, group), :]
        if group < lanes:
            block = jnp.concatenate([block] * (lanes // group), axis=0)
        held[:, row, :] = jnp.transpose(block)
    x = held[...]
    n = x.shape[0]
    for axis, shift in steps:
        partner = pltpu.roll(x, shift, axis)
        flipped = jnp.stack([partner[n - 1 - r] for r in range(n)], axis=0)
        x = jnp.maximum(x, flipped)
        j = n // 2
        while j >= 1:
            x = compare_split(x, 0, j)
            j //= 2
    held[...] = x
    o_ref[...] = jnp.transpose(held[:, 0, :])[: o_ref.shape[0]]


def merge_lists(x, steps, width):
    sublanes, lanes = 8, 128
    rank = x.shape[1]
    return pl.pallas_call(
        lambda *refs: merge_kernel(steps, *refs),
        out_shape=jax.ShapeDtypeStruct((width, rank), x.dtype),
        in_specs=[pl.BlockSpec(memory_space=pltpu.VMEM)],
        out_specs=pl.BlockSpec(memory_space=pltpu.VMEM),
        scratch_shapes=[pltpu.VMEM((rank, sublanes, lanes), x.dtype)],
    )(x)


def one_hot_take(table, index):
    ids = jnp.arange(table.shape[0], dtype=jnp.int32)
    hit = index[..., None] == ids
    return jnp.sum(jnp.where(hit, table, 0), axis=-1)


def body(
    item_feats,
    w_hidden,
    b_hidden,
    w_out,
    item_cluster,
    cluster_slot,
    catalog,
    cluster_fill,
    queries,
    probes,
):
    feat_count = lax.axis_size("feat")
    owner_count = lax.axis_size("clus")
    sizes = {"feat": feat_count, "clus": owner_count}
    feat_index = lax.axis_index("feat")
    owner_index = lax.axis_index("clus")
    device_rows = item_feats.shape[0] // feat_count
    emb_width = queries.shape[1]
    owned_count, row_dev = catalog.shape[:2]
    query_count = queries.shape[0]
    probe_count = probes.shape[1]

    probe_places = one_hot_take(cluster_slot, probes)
    probe_row = probe_places.reshape(-1, emb_width).astype(jnp.bfloat16)
    probe_lines = probe_row.shape[0]
    asked = jnp.concatenate([queries, probe_row], axis=0)
    lanes = 128
    asks, feats_all = exchange(
        [(asked, "clus", True), (item_feats.reshape(-1, lanes), "feat", True)], AXES, sizes, 0
    )

    feats_all = feats_all.reshape((feat_count,) + item_feats.shape)
    feats = jnp.transpose(feats_all, (1, 0, 2)).reshape(feats_all.shape[1], -1)
    pre_act = jnp.dot(feats, w_hidden, preferred_element_type=jnp.float32)
    hidden = jax.nn.silu(pre_act + b_hidden.astype(jnp.float32)).astype(jnp.bfloat16)
    partial = jnp.dot(hidden, w_out, preferred_element_type=jnp.float32)
    (parts,) = exchange(
        [(partial.reshape(feat_count, device_rows, -1), "feat", False)], AXES, sizes, 1
    )
    projected = jnp.sum(parts, axis=0)
    scaling = lax.rsqrt(jnp.mean(projected * projected, axis=1, keepdims=True) + 1e-06) * unit_scale
    embedded = (projected * scaling).astype(jnp.bfloat16)

    my_clusters = lax.dynamic_slice_in_dim(item_cluster, feat_index * device_rows, device_rows, 0)
    my_places = one_hot_take(cluster_slot, my_clusters)
    all_queries = asks[:, :query_count].reshape(-1, emb_width)
    all_probes = (
        asks[:, query_count : query_count + probe_lines]
        .astype(jnp.int32)
        .reshape(owner_count * query_count, probe_count)
    )

    first_owned = owner_index * owned_count
    local_ids = jnp.arange(owned_count, dtype=jnp.int32)
    owned_ids = first_owned + local_ids
    row_number = feat_index * row_dev + jnp.arange(row_dev, dtype=jnp.int32)
    stored_live = row_number[None, :] < cluster_fill[:, None]
    probed = jnp.any(all_probes[:, :, None] == owned_ids[None, None, :], axis=1)
    stored_allowed = (jnp.transpose(probed)[:, None, :] & stored_live[:, :, None]).reshape(
        owned_count * row_dev, -1
    )
    fresh_allowed = jnp.any(
        my_places[:, None, None] == jnp.transpose(all_probes)[None, :, :], axis=1
    )
    pad_rows = 2 * TOPK - owned_count * row_dev - device_rows
    allowed = jnp.concatenate(
        [stored_allowed, fresh_allowed, jnp.zeros((pad_rows, stored_allowed.shape[1]), bool)],
        axis=0,
    )
    scored_rows = jnp.concatenate(
        [
            catalog.reshape(owned_count * row_dev, emb_width),
            embedded,
            jnp.zeros((pad_rows, emb_width), embedded.dtype),
        ],
        0,
    )
    scores = jnp.einsum("rd,bd->rb", scored_rows, all_queries, preferred_element_type=jnp.float32)
    scores = jnp.where(allowed, scores, masked_score)
    local_best = top_half(scores)

    (arrived,) = exchange(
        [(local_best.reshape(owner_count, query_count, -1), "clus", False)], AXES, sizes, 3
    )
    sublanes, lanes = 8, 128
    groups = lanes // query_count
    steps = [(2, query_count * 2**i) for i in range(groups.bit_length() - 1)]
    steps += [(1, 2**i) for i in range(sublanes.bit_length() - 1)]
    narrowed = merge_lists(arrived.reshape(-1, arrived.shape[2]), tuple(steps), query_count)
    (gathered,) = exchange([(narrowed, "feat", True)], AXES, sizes, 4)
    steps = [(1, 2**i) for i in range(feat_count.bit_length() - 1)]
    return merge_lists(gathered.reshape(-1, gathered.shape[2]), tuple(steps), query_count)


def solution(mesh):
    return jax.shard_map(
        body,
        mesh=mesh,
        in_specs=(
            P("clus", "feat"),
            P(None, "feat"),
            P("feat"),
            P("feat", None),
            P("clus"),
            P(),
            P("clus", "feat", None),
            P("clus"),
            P("clus", None),
            P("clus", None),
        ),
        out_specs=P("clus", None),
        check_vma=False,
    )
```

```python
import jax
import jax.numpy as jnp
from jax import lax
from jax.experimental import pallas as pl
from jax.experimental.pallas import tpu as pltpu
from jax.sharding import PartitionSpec as P

TOPK = 128


masked_score = -1e30
unit_scale = 0.0625
AXES = ("feat", "clus")

MESH = pl.DeviceIdType.MESH


def exchange(jobs, axes, sizes, collective_id):
    count = len(jobs)
    widest = max(sizes[axis] for _, axis, _ in jobs)
    used_axes = sorted({axis for _, axis, _ in jobs}, key=axes.index)
    shapes = []
    for x, axis, spread in jobs:
        shape = ((sizes[axis],) + x.shape) if spread else x.shape
        shapes.append(jax.ShapeDtypeStruct(shape, x.dtype))

    def kernel(*refs):
        ins, outs = refs[:count], refs[count : 2 * count]
        send_sem, recv_sem, own_sem = refs[2 * count :]
        where = {a: lax.axis_index(a) for a in axes}

        def device(axis, peer):
            return tuple(peer if a == axis else where[a] for a in axes)

        barrier = pltpu.get_barrier_semaphore()
        peers = 0
        for axis in used_axes:
            n = sizes[axis]
            for step in range(1, n):
                pl.semaphore_signal(
                    barrier,
                    inc=1,
                    device_id=device(axis, lax.rem(where[axis] + step, n)),
                    device_id_type=MESH,
                )
            peers += n - 1
        pl.semaphore_wait(barrier, peers)
        started = []
        locals_ = []
        for job, (x, axis, spread) in enumerate(jobs):
            n = sizes[axis]
            me = where[axis]
            src_of = (lambda d, job=job: ins[job]) if spread else (lambda d, job=job: ins[job].at[d])
            own = pltpu.make_async_copy(src_of(me), outs[job].at[me], own_sem.at[job])
            own.start()
            locals_.append(own)
            for step in range(1, n):
                peer = lax.rem(me + step, n)
                copy = pltpu.make_async_remote_copy(
                    src_ref=src_of(peer),
                    dst_ref=outs[job].at[me],
                    send_sem=send_sem.at[job, step],
                    recv_sem=recv_sem.at[job, step],
                    device_id=device(axis, peer),
                    device_id_type=MESH,
                )
                copy.start()
                started.append(copy)
        for copy in started:
            copy.wait_send()
        for copy in locals_:
            copy.wait()
        for job, (x, axis, spread) in enumerate(jobs):
            n = sizes[axis]
            me = where[axis]
            src_of = (lambda d, job=job: ins[job]) if spread else (lambda d, job=job: ins[job].at[d])
            for step in range(1, n):
                source = lax.rem(me + n - step, n)
                pltpu.make_async_copy(
                    src_of(source), outs[job].at[source], recv_sem.at[job, step]
                ).wait()

    return pl.pallas_call(
        kernel,
        out_shape=tuple(shapes),
        in_specs=[pl.BlockSpec(memory_space=pl.ANY)] * count,
        out_specs=tuple(pl.BlockSpec(memory_space=pl.ANY) for _ in jobs),
        scratch_shapes=[
            pltpu.SemaphoreType.DMA((count, widest)),
            pltpu.SemaphoreType.DMA((count, widest)),
            pltpu.SemaphoreType.DMA((count,)),
        ],
        compiler_params=pltpu.CompilerParams(collective_id=collective_id, has_side_effects=True),
    )(*[x for x, _, _ in jobs])


def compare_split(x, k, j):
    n = x.shape[0]
    tile = x.shape[1:]
    if k == 0:
        v = x.reshape((n // (2 * j), 2, j) + tile)
        a, b = v[:, 0], v[:, 1]
        return jnp.stack([jnp.maximum(a, b), jnp.minimum(a, b)], axis=1).reshape(x.shape)
    v = x.reshape((n // (2 * k), 2, k // (2 * j), 2, j) + tile)
    up_a, up_b = v[:, 0, :, 0], v[:, 0, :, 1]
    down_a, down_b = v[:, 1, :, 0], v[:, 1, :, 1]
    up = jnp.stack([jnp.minimum(up_a, up_b), jnp.maximum(up_a, up_b)], axis=2)
    down = jnp.stack([jnp.maximum(down_a, down_b), jnp.minimum(down_a, down_b)], axis=2)
    return jnp.stack([up, down], axis=1).reshape(x.shape)


def top_half_kernel(x_ref, o_ref, spread, held):
    lanes = o_ref.shape[1]
    sublanes = spread.shape[1]
    for row in range(sublanes):
        spread[:, row, :] = x_ref[:, pl.ds(row * lanes, lanes)]
    x = spread[...]
    n = x.shape[0]
    half = n // 2
    k = 2
    while k <= half:
        j = k // 2
        while j >= 1:
            x = compare_split(x, k, j)
            j //= 2
        k *= 2
    x = jnp.maximum(x[:half], x[half:])
    j = half // 2
    while j >= 1:
        x = compare_split(x, 0, j)
        j //= 2
    held[...] = x
    for row in range(sublanes):
        o_ref[pl.ds(row * lanes, lanes), :] = jnp.transpose(held[:, row, :])


def top_half(x):
    n, width = x.shape
    sublanes = 8
    lanes = width // sublanes
    return pl.pallas_call(
        top_half_kernel,
        out_shape=jax.ShapeDtypeStruct((width, n // 2), x.dtype),
        in_specs=[pl.BlockSpec(memory_space=pltpu.VMEM)],
        out_specs=pl.BlockSpec(memory_space=pltpu.VMEM),
        scratch_shapes=[
            pltpu.VMEM((n, sublanes, lanes), x.dtype),
            pltpu.VMEM((n // 2, sublanes, lanes), x.dtype),
        ],
    )(x)


def merge_kernel(steps, x_ref, o_ref, held):
    sublanes, lanes = held.shape[1], held.shape[2]
    group = x_ref.shape[0] // sublanes
    for row in range(sublanes):
        block = x_ref[pl.ds(row * group, group), :]
        if group < lanes:
            block = jnp.concatenate([block] * (lanes // group), axis=0)
        held[:, row, :] = jnp.transpose(block)
    x = held[...]
    n = x.shape[0]
    for axis, shift in steps:
        partner = pltpu.roll(x, shift, axis)
        flipped = jnp.stack([partner[n - 1 - r] for r in range(n)], axis=0)
        x = jnp.maximum(x, flipped)
        j = n // 2
        while j >= 1:
            x = compare_split(x, 0, j)
            j //= 2
    held[...] = x
    o_ref[...] = jnp.transpose(held[:, 0, :])[: o_ref.shape[0]]


def merge_lists(x, steps, width):
    sublanes, lanes = 8, 128
    rank = x.shape[1]
    return pl.pallas_call(
        lambda *refs: merge_kernel(steps, *refs),
        out_shape=jax.ShapeDtypeStruct((width, rank), x.dtype),
        in_specs=[pl.BlockSpec(memory_space=pltpu.VMEM)],
        out_specs=pl.BlockSpec(memory_space=pltpu.VMEM),
        scratch_shapes=[pltpu.VMEM((rank, sublanes, lanes), x.dtype)],
    )(x)


def one_hot_take(table, index):
    ids = jnp.arange(table.shape[0], dtype=jnp.int32)
    hit = index[..., None] == ids
    return jnp.sum(jnp.where(hit, table, 0), axis=-1)


def body(
    item_feats,
    w_hidden,
    b_hidden,
    w_out,
    item_cluster,
    cluster_slot,
    catalog,
    cluster_fill,
    queries,
    probes,
):
    feat_count = lax.axis_size("feat")
    owner_count = lax.axis_size("clus")
    sizes = {"feat": feat_count, "clus": owner_count}
    feat_index = lax.axis_index("feat")
    owner_index = lax.axis_index("clus")
    device_rows = item_feats.shape[0] // feat_count
    emb_width = queries.shape[1]
    owned_count, row_dev = catalog.shape[:2]
    query_count = queries.shape[0]
    probe_count = probes.shape[1]

    probe_hot = probes[..., None] == jnp.arange(cluster_slot.shape[0], dtype=jnp.int32)
    probe_places = jnp.dot(
        probe_hot.astype(jnp.bfloat16),
        cluster_slot.astype(jnp.bfloat16),
        preferred_element_type=jnp.float32,
    )
    probe_row = probe_places.reshape(-1, emb_width).astype(jnp.bfloat16)
    probe_lines = probe_row.shape[0]
    asked = jnp.concatenate([queries, probe_row], axis=0)
    asks, feats_all = exchange(
        [(asked, "clus", True), (item_feats, "feat", True)], AXES, sizes, 0
    )

    pre_act = jnp.einsum(
        "sik,skh->ih",
        feats_all,
        w_hidden.reshape(feat_count, -1, w_hidden.shape[1]),
        preferred_element_type=jnp.float32,
    )
    hidden = jax.nn.silu(pre_act + b_hidden.astype(jnp.float32)).astype(jnp.bfloat16)
    partial = jnp.dot(hidden, w_out, preferred_element_type=jnp.float32)
    (parts,) = exchange(
        [(partial.reshape(feat_count, device_rows, -1), "feat", False)], AXES, sizes, 1
    )
    projected = jnp.sum(parts, axis=0)
    scaling = lax.rsqrt(jnp.mean(projected * projected, axis=1, keepdims=True) + 1e-06) * unit_scale
    embedded = (projected * scaling).astype(jnp.bfloat16)

    my_clusters = lax.dynamic_slice_in_dim(item_cluster, feat_index * device_rows, device_rows, 0)
    my_places = one_hot_take(cluster_slot, my_clusters)
    all_queries = asks[:, :query_count].reshape(-1, emb_width)
    all_probes = (
        asks[:, query_count : query_count + probe_lines]
        .astype(jnp.int32)
        .reshape(owner_count * query_count, probe_count)
    )

    first_owned = owner_index * owned_count
    local_ids = jnp.arange(owned_count, dtype=jnp.int32)
    owned_ids = first_owned + local_ids
    row_number = feat_index * row_dev + jnp.arange(row_dev, dtype=jnp.int32)
    stored_live = row_number[None, :] < cluster_fill[:, None]
    probed = jnp.any(all_probes[:, :, None] == owned_ids[None, None, :], axis=1)
    stored_allowed = (jnp.transpose(probed)[:, None, :] & stored_live[:, :, None]).reshape(
        owned_count * row_dev, -1
    )
    fresh_allowed = jnp.any(
        my_places[:, None, None] == jnp.transpose(all_probes)[None, :, :], axis=1
    )
    pad_rows = 2 * TOPK - owned_count * row_dev - device_rows
    allowed = jnp.concatenate(
        [stored_allowed, fresh_allowed, jnp.zeros((pad_rows, stored_allowed.shape[1]), bool)],
        axis=0,
    )
    scored_rows = jnp.concatenate(
        [
            catalog.reshape(owned_count * row_dev, emb_width),
            embedded,
            jnp.zeros((pad_rows, emb_width), embedded.dtype),
        ],
        0,
    )
    scores = jnp.einsum("rd,bd->rb", scored_rows, all_queries, preferred_element_type=jnp.float32)
    scores = jnp.where(allowed, scores, masked_score)
    local_best = top_half(scores)

    (arrived,) = exchange(
        [(local_best.reshape(owner_count, query_count, -1), "clus", False)], AXES, sizes, 3
    )
    sublanes, lanes = 8, 128
    groups = lanes // query_count
    steps = [(2, query_count * 2**i) for i in range(groups.bit_length() - 1)]
    steps += [(1, 2**i) for i in range(sublanes.bit_length() - 1)]
    narrowed = merge_lists(arrived.reshape(-1, arrived.shape[2]), tuple(steps), query_count)
    (gathered,) = exchange([(narrowed, "feat", True)], AXES, sizes, 4)
    steps = [(1, 2**i) for i in range(feat_count.bit_length() - 1)]
    return merge_lists(gathered.reshape(-1, gathered.shape[2]), tuple(steps), query_count)


def solution(mesh):
    return jax.shard_map(
        body,
        mesh=mesh,
        in_specs=(
            P("clus", "feat"),
            P(None, "feat"),
            P("feat"),
            P("feat", None),
            P("clus"),
            P(),
            P("clus", "feat", None),
            P("clus"),
            P("clus", None),
            P("clus", None),
        ),
        out_specs=P("clus", None),
        check_vma=False,
    )
```

```python
import jax
import jax.numpy as jnp
from jax import lax
from jax.experimental import pallas as pl
from jax.experimental.pallas import tpu as pltpu
from jax.sharding import PartitionSpec as P

TOPK = 128


masked_score = -1e30
unit_scale = 0.0625
AXES = ("feat", "clus")

MESH = pl.DeviceIdType.MESH


def exchange(jobs, axes, sizes, collective_id):
    count = len(jobs)
    widest = max(sizes[axis] for _, axis, _ in jobs)
    used_axes = sorted({axis for _, axis, _ in jobs}, key=axes.index)
    shapes = []
    for x, axis, spread in jobs:
        shape = ((sizes[axis],) + x.shape) if spread else x.shape
        shapes.append(jax.ShapeDtypeStruct(shape, x.dtype))

    def kernel(*refs):
        ins, outs = refs[:count], refs[count : 2 * count]
        send_sem, recv_sem, own_sem = refs[2 * count :]
        where = {a: lax.axis_index(a) for a in axes}

        def device(axis, peer):
            return tuple(peer if a == axis else where[a] for a in axes)

        barrier = pltpu.get_barrier_semaphore()
        peers = 0
        for axis in used_axes:
            n = sizes[axis]
            for step in range(1, n):
                pl.semaphore_signal(
                    barrier,
                    inc=1,
                    device_id=device(axis, lax.rem(where[axis] + step, n)),
                    device_id_type=MESH,
                )
            peers += n - 1
        pl.semaphore_wait(barrier, peers)
        started = []
        locals_ = []
        for job, (x, axis, spread) in enumerate(jobs):
            n = sizes[axis]
            me = where[axis]
            src_of = (lambda d, job=job: ins[job]) if spread else (lambda d, job=job: ins[job].at[d])
            own = pltpu.make_async_copy(src_of(me), outs[job].at[me], own_sem.at[job])
            own.start()
            locals_.append(own)
            for step in range(1, n):
                peer = lax.rem(me + step, n)
                copy = pltpu.make_async_remote_copy(
                    src_ref=src_of(peer),
                    dst_ref=outs[job].at[me],
                    send_sem=send_sem.at[job, step],
                    recv_sem=recv_sem.at[job, step],
                    device_id=device(axis, peer),
                    device_id_type=MESH,
                )
                copy.start()
                started.append(copy)
        for copy in started:
            copy.wait_send()
        for copy in locals_:
            copy.wait()
        for job, (x, axis, spread) in enumerate(jobs):
            n = sizes[axis]
            me = where[axis]
            src_of = (lambda d, job=job: ins[job]) if spread else (lambda d, job=job: ins[job].at[d])
            for step in range(1, n):
                source = lax.rem(me + n - step, n)
                pltpu.make_async_copy(
                    src_of(source), outs[job].at[source], recv_sem.at[job, step]
                ).wait()

    return pl.pallas_call(
        kernel,
        out_shape=tuple(shapes),
        in_specs=[pl.BlockSpec(memory_space=pl.ANY)] * count,
        out_specs=tuple(pl.BlockSpec(memory_space=pl.ANY) for _ in jobs),
        scratch_shapes=[
            pltpu.SemaphoreType.DMA((count, widest)),
            pltpu.SemaphoreType.DMA((count, widest)),
            pltpu.SemaphoreType.DMA((count,)),
        ],
        compiler_params=pltpu.CompilerParams(collective_id=collective_id, has_side_effects=True),
    )(*[x for x, _, _ in jobs])


def compare_split(x, k, j):
    n = x.shape[0]
    tile = x.shape[1:]
    if k == 0:
        v = x.reshape((n // (2 * j), 2, j) + tile)
        a, b = v[:, 0], v[:, 1]
        return jnp.stack([jnp.maximum(a, b), jnp.minimum(a, b)], axis=1).reshape(x.shape)
    v = x.reshape((n // (2 * k), 2, k // (2 * j), 2, j) + tile)
    up_a, up_b = v[:, 0, :, 0], v[:, 0, :, 1]
    down_a, down_b = v[:, 1, :, 0], v[:, 1, :, 1]
    up = jnp.stack([jnp.minimum(up_a, up_b), jnp.maximum(up_a, up_b)], axis=2)
    down = jnp.stack([jnp.maximum(down_a, down_b), jnp.minimum(down_a, down_b)], axis=2)
    return jnp.stack([up, down], axis=1).reshape(x.shape)


def top_half_kernel(x_ref, o_ref, spread, held):
    lanes = o_ref.shape[1]
    sublanes = spread.shape[1]
    for row in range(sublanes):
        spread[:, row, :] = x_ref[:, pl.ds(row * lanes, lanes)]
    x = spread[...]
    n = x.shape[0]
    half = n // 2
    k = 2
    while k <= half:
        j = k // 2
        while j >= 1:
            x = compare_split(x, k, j)
            j //= 2
        k *= 2
    x = jnp.maximum(x[:half], x[half:])
    j = half // 2
    while j >= 1:
        x = compare_split(x, 0, j)
        j //= 2
    held[...] = x
    for row in range(sublanes):
        o_ref[pl.ds(row * lanes, lanes), :] = jnp.transpose(held[:, row, :])


def top_half(x):
    n, width = x.shape
    sublanes = 8
    lanes = width // sublanes
    return pl.pallas_call(
        top_half_kernel,
        out_shape=jax.ShapeDtypeStruct((width, n // 2), x.dtype),
        in_specs=[pl.BlockSpec(memory_space=pltpu.VMEM)],
        out_specs=pl.BlockSpec(memory_space=pltpu.VMEM),
        scratch_shapes=[
            pltpu.VMEM((n, sublanes, lanes), x.dtype),
            pltpu.VMEM((n // 2, sublanes, lanes), x.dtype),
        ],
    )(x)


def merge_kernel(steps, x_ref, o_ref, held):
    sublanes, lanes = held.shape[1], held.shape[2]
    group = x_ref.shape[0] // sublanes
    for row in range(sublanes):
        block = x_ref[pl.ds(row * group, group), :]
        if group < lanes:
            block = jnp.concatenate([block] * (lanes // group), axis=0)
        held[:, row, :] = jnp.transpose(block)
    x = held[...]
    n = x.shape[0]
    for axis, shift in steps:
        partner = pltpu.roll(x, shift, axis)
        flipped = jnp.stack([partner[n - 1 - r] for r in range(n)], axis=0)
        x = jnp.maximum(x, flipped)
        j = n // 2
        while j >= 1:
            x = compare_split(x, 0, j)
            j //= 2
    held[...] = x
    o_ref[...] = jnp.transpose(held[:, 0, :])[: o_ref.shape[0]]


def merge_lists(x, steps, width):
    sublanes, lanes = 8, 128
    rank = x.shape[1]
    return pl.pallas_call(
        lambda *refs: merge_kernel(steps, *refs),
        out_shape=jax.ShapeDtypeStruct((width, rank), x.dtype),
        in_specs=[pl.BlockSpec(memory_space=pltpu.VMEM)],
        out_specs=pl.BlockSpec(memory_space=pltpu.VMEM),
        scratch_shapes=[pltpu.VMEM((rank, sublanes, lanes), x.dtype)],
    )(x)


def one_hot_take(table, index):
    ids = jnp.arange(table.shape[0], dtype=jnp.int32)
    hit = index[..., None] == ids
    return jnp.sum(jnp.where(hit, table, 0), axis=-1)


def body(
    item_feats,
    w_hidden,
    b_hidden,
    w_out,
    item_cluster,
    cluster_slot,
    catalog,
    cluster_fill,
    queries,
    probes,
):
    feat_count = lax.axis_size("feat")
    owner_count = lax.axis_size("clus")
    sizes = {"feat": feat_count, "clus": owner_count}
    feat_index = lax.axis_index("feat")
    owner_index = lax.axis_index("clus")
    device_rows = item_feats.shape[0] // feat_count
    emb_width = queries.shape[1]
    owned_count, row_dev = catalog.shape[:2]
    query_count = queries.shape[0]
    probe_count = probes.shape[1]

    probe_hot = probes[..., None] == jnp.arange(cluster_slot.shape[0], dtype=jnp.int32)
    probe_places = jnp.dot(
        probe_hot.astype(jnp.bfloat16),
        cluster_slot.astype(jnp.bfloat16),
        preferred_element_type=jnp.float32,
    )
    probe_row = probe_places.reshape(-1, emb_width).astype(jnp.bfloat16)
    probe_lines = probe_row.shape[0]
    asked = jnp.concatenate([queries, probe_row], axis=0)
    asks, feats_all = exchange(
        [(asked, "clus", True), (jnp.transpose(item_feats), "feat", True)], AXES, sizes, 0
    )

    pre_act = jnp.einsum(
        "ski,skh->ih",
        feats_all,
        w_hidden.reshape(feat_count, -1, w_hidden.shape[1]),
        preferred_element_type=jnp.float32,
    )
    hidden = jax.nn.silu(pre_act + b_hidden.astype(jnp.float32)).astype(jnp.bfloat16)
    partial = jnp.dot(hidden, w_out, preferred_element_type=jnp.float32)
    (parts,) = exchange(
        [(partial.reshape(feat_count, device_rows, -1), "feat", False)], AXES, sizes, 1
    )
    projected = jnp.sum(parts, axis=0)
    scaling = lax.rsqrt(jnp.mean(projected * projected, axis=1, keepdims=True) + 1e-06) * unit_scale
    embedded = (projected * scaling).astype(jnp.bfloat16)

    my_clusters = lax.dynamic_slice_in_dim(item_cluster, feat_index * device_rows, device_rows, 0)
    my_places = one_hot_take(cluster_slot, my_clusters)
    all_queries = asks[:, :query_count].reshape(-1, emb_width)
    all_probes = (
        asks[:, query_count : query_count + probe_lines]
        .astype(jnp.int32)
        .reshape(owner_count * query_count, probe_count)
    )

    first_owned = owner_index * owned_count
    local_ids = jnp.arange(owned_count, dtype=jnp.int32)
    owned_ids = first_owned + local_ids
    row_number = feat_index * row_dev + jnp.arange(row_dev, dtype=jnp.int32)
    stored_live = row_number[None, :] < cluster_fill[:, None]
    probed = jnp.any(all_probes[:, :, None] == owned_ids[None, None, :], axis=1)
    stored_allowed = (jnp.transpose(probed)[:, None, :] & stored_live[:, :, None]).reshape(
        owned_count * row_dev, -1
    )
    fresh_allowed = jnp.any(
        my_places[:, None, None] == jnp.transpose(all_probes)[None, :, :], axis=1
    )
    pad_rows = 2 * TOPK - owned_count * row_dev - device_rows
    allowed = jnp.concatenate(
        [stored_allowed, fresh_allowed, jnp.zeros((pad_rows, stored_allowed.shape[1]), bool)],
        axis=0,
    )
    scored_rows = jnp.concatenate(
        [
            catalog.reshape(owned_count * row_dev, emb_width),
            embedded,
            jnp.zeros((pad_rows, emb_width), embedded.dtype),
        ],
        0,
    )
    scores = jnp.einsum("rd,bd->rb", scored_rows, all_queries, preferred_element_type=jnp.float32)
    scores = jnp.where(allowed, scores, masked_score)
    local_best = top_half(scores)

    (arrived,) = exchange(
        [(local_best.reshape(owner_count, query_count, -1), "clus", False)], AXES, sizes, 3
    )
    sublanes, lanes = 8, 128
    groups = lanes // query_count
    steps = [(2, query_count * 2**i) for i in range(groups.bit_length() - 1)]
    steps += [(1, 2**i) for i in range(sublanes.bit_length() - 1)]
    narrowed = merge_lists(arrived.reshape(-1, arrived.shape[2]), tuple(steps), query_count)
    (gathered,) = exchange([(narrowed, "feat", True)], AXES, sizes, 4)
    steps = [(1, 2**i) for i in range(feat_count.bit_length() - 1)]
    return merge_lists(gathered.reshape(-1, gathered.shape[2]), tuple(steps), query_count)


def solution(mesh):
    return jax.shard_map(
        body,
        mesh=mesh,
        in_specs=(
            P("clus", "feat"),
            P(None, "feat"),
            P("feat"),
            P("feat", None),
            P("clus"),
            P(),
            P("clus", "feat", None),
            P("clus"),
            P("clus", None),
            P("clus", None),
        ),
        out_specs=P("clus", None),
        check_vma=False,
    )
```

```python
import jax
import jax.numpy as jnp
from jax import lax
from jax.experimental import pallas as pl
from jax.experimental.pallas import tpu as pltpu
from jax.sharding import PartitionSpec as P

TOPK = 128


masked_score = -1e30
unit_scale = 0.0625
AXES = ("feat", "clus")

MESH = pl.DeviceIdType.MESH


def exchange(jobs, axes, sizes, collective_id):
    count = len(jobs)
    widest = max(sizes[axis] for _, axis, _ in jobs)
    used_axes = sorted({axis for _, axis, _ in jobs}, key=axes.index)
    shapes = []
    for x, axis, spread in jobs:
        shape = ((sizes[axis],) + x.shape) if spread else x.shape
        shapes.append(jax.ShapeDtypeStruct(shape, x.dtype))

    def kernel(*refs):
        ins, outs = refs[:count], refs[count : 2 * count]
        send_sem, recv_sem, own_sem = refs[2 * count :]
        where = {a: lax.axis_index(a) for a in axes}

        def device(axis, peer):
            return tuple(peer if a == axis else where[a] for a in axes)

        barrier = pltpu.get_barrier_semaphore()
        peers = 0
        for axis in used_axes:
            n = sizes[axis]
            for step in range(1, n):
                pl.semaphore_signal(
                    barrier,
                    inc=1,
                    device_id=device(axis, lax.rem(where[axis] + step, n)),
                    device_id_type=MESH,
                )
            peers += n - 1
        pl.semaphore_wait(barrier, peers)
        started = []
        locals_ = []
        for job, (x, axis, spread) in enumerate(jobs):
            n = sizes[axis]
            me = where[axis]
            src_of = (lambda d, job=job: ins[job]) if spread else (lambda d, job=job: ins[job].at[d])
            own = pltpu.make_async_copy(src_of(me), outs[job].at[me], own_sem.at[job])
            own.start()
            locals_.append(own)
            for step in range(1, n):
                peer = lax.rem(me + step, n)
                copy = pltpu.make_async_remote_copy(
                    src_ref=src_of(peer),
                    dst_ref=outs[job].at[me],
                    send_sem=send_sem.at[job, step],
                    recv_sem=recv_sem.at[job, step],
                    device_id=device(axis, peer),
                    device_id_type=MESH,
                )
                copy.start()
                started.append(copy)
        for copy in started:
            copy.wait_send()
        for copy in locals_:
            copy.wait()
        for job, (x, axis, spread) in enumerate(jobs):
            n = sizes[axis]
            me = where[axis]
            src_of = (lambda d, job=job: ins[job]) if spread else (lambda d, job=job: ins[job].at[d])
            for step in range(1, n):
                source = lax.rem(me + n - step, n)
                pltpu.make_async_copy(
                    src_of(source), outs[job].at[source], recv_sem.at[job, step]
                ).wait()

    return pl.pallas_call(
        kernel,
        out_shape=tuple(shapes),
        in_specs=[pl.BlockSpec(memory_space=pl.ANY)] * count,
        out_specs=tuple(pl.BlockSpec(memory_space=pl.ANY) for _ in jobs),
        scratch_shapes=[
            pltpu.SemaphoreType.DMA((count, widest)),
            pltpu.SemaphoreType.DMA((count, widest)),
            pltpu.SemaphoreType.DMA((count,)),
        ],
        compiler_params=pltpu.CompilerParams(collective_id=collective_id, has_side_effects=True),
    )(*[x for x, _, _ in jobs])


def compare_split(x, k, j):
    n = x.shape[0]
    tile = x.shape[1:]
    if k == 0:
        v = x.reshape((n // (2 * j), 2, j) + tile)
        a, b = v[:, 0], v[:, 1]
        return jnp.stack([jnp.maximum(a, b), jnp.minimum(a, b)], axis=1).reshape(x.shape)
    v = x.reshape((n // (2 * k), 2, k // (2 * j), 2, j) + tile)
    up_a, up_b = v[:, 0, :, 0], v[:, 0, :, 1]
    down_a, down_b = v[:, 1, :, 0], v[:, 1, :, 1]
    up = jnp.stack([jnp.minimum(up_a, up_b), jnp.maximum(up_a, up_b)], axis=2)
    down = jnp.stack([jnp.maximum(down_a, down_b), jnp.minimum(down_a, down_b)], axis=2)
    return jnp.stack([up, down], axis=1).reshape(x.shape)


def top_half_kernel(x_ref, o_ref, spread, held):
    lanes = o_ref.shape[1]
    sublanes = spread.shape[1]
    for row in range(sublanes):
        spread[:, row, :] = x_ref[:, pl.ds(row * lanes, lanes)]
    x = spread[...]
    n = x.shape[0]
    half = n // 2
    k = 2
    while k <= half:
        j = k // 2
        while j >= 1:
            x = compare_split(x, k, j)
            j //= 2
        k *= 2
    x = jnp.maximum(x[:half], x[half:])
    j = half // 2
    while j >= 1:
        x = compare_split(x, 0, j)
        j //= 2
    held[...] = x
    for row in range(sublanes):
        o_ref[pl.ds(row * lanes, lanes), :] = jnp.transpose(held[:, row, :])


def top_half(x):
    n, width = x.shape
    sublanes = 8
    lanes = width // sublanes
    return pl.pallas_call(
        top_half_kernel,
        out_shape=jax.ShapeDtypeStruct((width, n // 2), x.dtype),
        in_specs=[pl.BlockSpec(memory_space=pltpu.VMEM)],
        out_specs=pl.BlockSpec(memory_space=pltpu.VMEM),
        scratch_shapes=[
            pltpu.VMEM((n, sublanes, lanes), x.dtype),
            pltpu.VMEM((n // 2, sublanes, lanes), x.dtype),
        ],
    )(x)


def merge_kernel(steps, x_ref, o_ref, held):
    sublanes, lanes = held.shape[1], held.shape[2]
    group = x_ref.shape[0] // sublanes
    for row in range(sublanes):
        block = x_ref[pl.ds(row * group, group), :]
        if group < lanes:
            block = jnp.concatenate([block] * (lanes // group), axis=0)
        held[:, row, :] = jnp.transpose(block)
    x = held[...]
    n = x.shape[0]
    for axis, shift in steps:
        partner = pltpu.roll(x, shift, axis)
        flipped = jnp.stack([partner[n - 1 - r] for r in range(n)], axis=0)
        x = jnp.maximum(x, flipped)
        j = n // 2
        while j >= 1:
            x = compare_split(x, 0, j)
            j //= 2
    held[...] = x
    o_ref[...] = jnp.transpose(held[:, 0, :])[: o_ref.shape[0]]


def merge_lists(x, steps, width):
    sublanes, lanes = 8, 128
    rank = x.shape[1]
    return pl.pallas_call(
        lambda *refs: merge_kernel(steps, *refs),
        out_shape=jax.ShapeDtypeStruct((width, rank), x.dtype),
        in_specs=[pl.BlockSpec(memory_space=pltpu.VMEM)],
        out_specs=pl.BlockSpec(memory_space=pltpu.VMEM),
        scratch_shapes=[pltpu.VMEM((rank, sublanes, lanes), x.dtype)],
    )(x)


def one_hot_take(table, index):
    ids = jnp.arange(table.shape[0], dtype=jnp.int32)
    hit = index[..., None] == ids
    return jnp.sum(jnp.where(hit, table, 0), axis=-1)


def body(
    item_feats,
    w_hidden,
    b_hidden,
    w_out,
    item_cluster,
    cluster_slot,
    catalog,
    cluster_fill,
    queries,
    probes,
):
    feat_count = lax.axis_size("feat")
    owner_count = lax.axis_size("clus")
    sizes = {"feat": feat_count, "clus": owner_count}
    feat_index = lax.axis_index("feat")
    owner_index = lax.axis_index("clus")
    device_rows = item_feats.shape[0] // feat_count
    emb_width = queries.shape[1]
    owned_count, row_dev = catalog.shape[:2]
    query_count = queries.shape[0]
    probe_count = probes.shape[1]

    probe_row = jnp.transpose(probes).reshape(-1, emb_width).astype(jnp.bfloat16)
    probe_lines = probe_row.shape[0]
    asked = jnp.concatenate([queries, probe_row], axis=0)
    asks, feats_all = exchange(
        [(asked, "clus", True), (jnp.transpose(item_feats), "feat", True)], AXES, sizes, 0
    )

    pre_act = jnp.einsum(
        "ski,skh->ih",
        feats_all,
        w_hidden.reshape(feat_count, -1, w_hidden.shape[1]),
        preferred_element_type=jnp.float32,
    )
    hidden = jax.nn.silu(pre_act + b_hidden.astype(jnp.float32)).astype(jnp.bfloat16)
    partial = jnp.dot(hidden, w_out, preferred_element_type=jnp.float32)
    (parts,) = exchange(
        [(partial.reshape(feat_count, device_rows, -1), "feat", False)], AXES, sizes, 1
    )
    projected = jnp.sum(parts, axis=0)
    scaling = lax.rsqrt(jnp.mean(projected * projected, axis=1, keepdims=True) + 1e-06) * unit_scale
    embedded = (projected * scaling).astype(jnp.bfloat16)

    my_clusters = lax.dynamic_slice_in_dim(item_cluster, feat_index * device_rows, device_rows, 0)
    all_queries = asks[:, :query_count].reshape(-1, emb_width)
    all_probes = (
        asks[:, query_count : query_count + probe_lines]
        .astype(jnp.int32)
        .reshape(owner_count, probe_count, query_count)
    )

    first_owned = owner_index * owned_count
    local_ids = jnp.arange(owned_count, dtype=jnp.int32)
    owned_ids = first_owned + local_ids
    row_number = feat_index * row_dev + jnp.arange(row_dev, dtype=jnp.int32)
    stored_live = row_number[None, :] < cluster_fill[:, None]
    slot_ids = jnp.arange(cluster_slot.shape[0], dtype=jnp.int32)
    owned_clusters = jnp.sum(
        jnp.where(cluster_slot[None, :] == owned_ids[:, None], slot_ids[None, :], 0), axis=1
    )
    probed = jnp.any(all_probes[..., None] == owned_clusters, axis=1).reshape(-1, owned_count)
    stored_allowed = (jnp.transpose(probed)[:, None, :] & stored_live[:, :, None]).reshape(
        owned_count * row_dev, -1
    )
    fresh_allowed = jnp.any(
        my_clusters[:, None, None, None] == all_probes[None], axis=2
    ).reshape(device_rows, -1)
    pad_rows = 2 * TOPK - owned_count * row_dev - device_rows
    allowed = jnp.concatenate(
        [stored_allowed, fresh_allowed, jnp.zeros((pad_rows, stored_allowed.shape[1]), bool)],
        axis=0,
    )
    scored_rows = jnp.concatenate(
        [
            catalog.reshape(owned_count * row_dev, emb_width),
            embedded,
            jnp.zeros((pad_rows, emb_width), embedded.dtype),
        ],
        0,
    )
    scores = jnp.einsum("rd,bd->rb", scored_rows, all_queries, preferred_element_type=jnp.float32)
    scores = jnp.where(allowed, scores, masked_score)
    local_best = top_half(scores)

    (arrived,) = exchange(
        [(local_best.reshape(owner_count, query_count, -1), "clus", False)], AXES, sizes, 3
    )
    sublanes, lanes = 8, 128
    groups = lanes // query_count
    steps = [(2, query_count * 2**i) for i in range(groups.bit_length() - 1)]
    steps += [(1, 2**i) for i in range(sublanes.bit_length() - 1)]
    narrowed = merge_lists(arrived.reshape(-1, arrived.shape[2]), tuple(steps), query_count)
    (gathered,) = exchange([(narrowed, "feat", True)], AXES, sizes, 4)
    steps = [(1, 2**i) for i in range(feat_count.bit_length() - 1)]
    return merge_lists(gathered.reshape(-1, gathered.shape[2]), tuple(steps), query_count)


def solution(mesh):
    return jax.shard_map(
        body,
        mesh=mesh,
        in_specs=(
            P("clus", "feat"),
            P(None, "feat"),
            P("feat"),
            P("feat", None),
            P("clus"),
            P(),
            P("clus", "feat", None),
            P("clus"),
            P("clus", None),
            P("clus", None),
        ),
        out_specs=P("clus", None),
        check_vma=False,
    )
```

```python
import jax
import jax.numpy as jnp
from jax import lax
from jax.experimental import pallas as pl
from jax.experimental.pallas import tpu as pltpu
from jax.sharding import PartitionSpec as P

TOPK = 128


masked_score = -1e30
unit_scale = 0.0625
AXES = ("feat", "clus")

MESH = pl.DeviceIdType.MESH


def exchange(jobs, axes, sizes, collective_id):
    count = len(jobs)
    widest = max(sizes[axis] for _, axis, _ in jobs)
    used_axes = sorted({axis for _, axis, _ in jobs}, key=axes.index)
    shapes = []
    for x, axis, spread in jobs:
        shape = ((sizes[axis],) + x.shape) if spread else x.shape
        shapes.append(jax.ShapeDtypeStruct(shape, x.dtype))

    def kernel(*refs):
        ins, outs = refs[:count], refs[count : 2 * count]
        send_sem, recv_sem, own_sem = refs[2 * count :]
        where = {a: lax.axis_index(a) for a in axes}

        def device(axis, peer):
            return tuple(peer if a == axis else where[a] for a in axes)

        barrier = pltpu.get_barrier_semaphore()
        peers = 0
        for axis in used_axes:
            n = sizes[axis]
            for step in range(1, n):
                pl.semaphore_signal(
                    barrier,
                    inc=1,
                    device_id=device(axis, lax.rem(where[axis] + step, n)),
                    device_id_type=MESH,
                )
            peers += n - 1
        pl.semaphore_wait(barrier, peers)
        started = []
        locals_ = []
        for job, (x, axis, spread) in enumerate(jobs):
            n = sizes[axis]
            me = where[axis]
            src_of = (lambda d, job=job: ins[job]) if spread else (lambda d, job=job: ins[job].at[d])
            own = pltpu.make_async_copy(src_of(me), outs[job].at[me], own_sem.at[job])
            own.start()
            locals_.append(own)
            for step in range(1, n):
                peer = lax.rem(me + step, n)
                copy = pltpu.make_async_remote_copy(
                    src_ref=src_of(peer),
                    dst_ref=outs[job].at[me],
                    send_sem=send_sem.at[job, step],
                    recv_sem=recv_sem.at[job, step],
                    device_id=device(axis, peer),
                    device_id_type=MESH,
                )
                copy.start()
                started.append(copy)
        for copy in started:
            copy.wait_send()
        for copy in locals_:
            copy.wait()
        for job, (x, axis, spread) in enumerate(jobs):
            n = sizes[axis]
            me = where[axis]
            src_of = (lambda d, job=job: ins[job]) if spread else (lambda d, job=job: ins[job].at[d])
            for step in range(1, n):
                source = lax.rem(me + n - step, n)
                pltpu.make_async_copy(
                    src_of(source), outs[job].at[source], recv_sem.at[job, step]
                ).wait()

    return pl.pallas_call(
        kernel,
        out_shape=tuple(shapes),
        in_specs=[pl.BlockSpec(memory_space=pl.ANY)] * count,
        out_specs=tuple(pl.BlockSpec(memory_space=pl.ANY) for _ in jobs),
        scratch_shapes=[
            pltpu.SemaphoreType.DMA((count, widest)),
            pltpu.SemaphoreType.DMA((count, widest)),
            pltpu.SemaphoreType.DMA((count,)),
        ],
        compiler_params=pltpu.CompilerParams(collective_id=collective_id, has_side_effects=True),
    )(*[x for x, _, _ in jobs])


def compare_split(x, k, j):
    n = x.shape[0]
    tile = x.shape[1:]
    if k == 0:
        v = x.reshape((n // (2 * j), 2, j) + tile)
        a, b = v[:, 0], v[:, 1]
        return jnp.stack([jnp.maximum(a, b), jnp.minimum(a, b)], axis=1).reshape(x.shape)
    v = x.reshape((n // (2 * k), 2, k // (2 * j), 2, j) + tile)
    up_a, up_b = v[:, 0, :, 0], v[:, 0, :, 1]
    down_a, down_b = v[:, 1, :, 0], v[:, 1, :, 1]
    up = jnp.stack([jnp.minimum(up_a, up_b), jnp.maximum(up_a, up_b)], axis=2)
    down = jnp.stack([jnp.maximum(down_a, down_b), jnp.minimum(down_a, down_b)], axis=2)
    return jnp.stack([up, down], axis=1).reshape(x.shape)


def top_half_kernel(x_ref, o_ref, spread, held):
    lanes = o_ref.shape[1]
    sublanes = spread.shape[1]
    for row in range(sublanes):
        spread[:, row, :] = x_ref[:, pl.ds(row * lanes, lanes)]
    x = spread[...]
    n = x.shape[0]
    half = n // 2
    k = 2
    while k <= half:
        j = k // 2
        while j >= 1:
            x = compare_split(x, k, j)
            j //= 2
        k *= 2
    x = jnp.maximum(x[:half], x[half:])
    j = half // 2
    while j >= 1:
        x = compare_split(x, 0, j)
        j //= 2
    held[...] = x
    for row in range(sublanes):
        o_ref[pl.ds(row * lanes, lanes), :] = jnp.transpose(held[:, row, :])


def top_half(x):
    n, width = x.shape
    sublanes = 8
    lanes = width // sublanes
    return pl.pallas_call(
        top_half_kernel,
        out_shape=jax.ShapeDtypeStruct((width, n // 2), x.dtype),
        in_specs=[pl.BlockSpec(memory_space=pltpu.VMEM)],
        out_specs=pl.BlockSpec(memory_space=pltpu.VMEM),
        scratch_shapes=[
            pltpu.VMEM((n, sublanes, lanes), x.dtype),
            pltpu.VMEM((n // 2, sublanes, lanes), x.dtype),
        ],
    )(x)


def merge_kernel(steps, x_ref, o_ref, held):
    sublanes, lanes = held.shape[1], held.shape[2]
    group = x_ref.shape[0] // sublanes
    for row in range(sublanes):
        block = x_ref[pl.ds(row * group, group), :]
        if group < lanes:
            block = jnp.concatenate([block] * (lanes // group), axis=0)
        held[:, row, :] = jnp.transpose(block)
    x = held[...]
    n = x.shape[0]
    for axis, shift in steps:
        partner = pltpu.roll(x, shift, axis)
        flipped = jnp.stack([partner[n - 1 - r] for r in range(n)], axis=0)
        x = jnp.maximum(x, flipped)
        j = n // 2
        while j >= 1:
            x = compare_split(x, 0, j)
            j //= 2
    held[...] = x
    o_ref[...] = jnp.transpose(held[:, 0, :])[: o_ref.shape[0]]


def merge_lists(x, steps, width):
    sublanes, lanes = 8, 128
    rank = x.shape[1]
    return pl.pallas_call(
        lambda *refs: merge_kernel(steps, *refs),
        out_shape=jax.ShapeDtypeStruct((width, rank), x.dtype),
        in_specs=[pl.BlockSpec(memory_space=pltpu.VMEM)],
        out_specs=pl.BlockSpec(memory_space=pltpu.VMEM),
        scratch_shapes=[pltpu.VMEM((rank, sublanes, lanes), x.dtype)],
    )(x)


def one_hot_take(table, index):
    ids = jnp.arange(table.shape[0], dtype=jnp.int32)
    hit = index[..., None] == ids
    return jnp.sum(jnp.where(hit, table, 0), axis=-1)


def body(
    item_feats,
    w_hidden,
    b_hidden,
    w_out,
    item_cluster,
    cluster_slot,
    catalog,
    cluster_fill,
    queries,
    probes,
):
    feat_count = lax.axis_size("feat")
    owner_count = lax.axis_size("clus")
    sizes = {"feat": feat_count, "clus": owner_count}
    feat_index = lax.axis_index("feat")
    owner_index = lax.axis_index("clus")
    device_rows = item_feats.shape[0] // feat_count
    emb_width = queries.shape[1]
    owned_count, row_dev = catalog.shape[:2]
    query_count = queries.shape[0]
    probe_count = probes.shape[1]

    probe_row = jnp.transpose(probes).reshape(-1, emb_width).astype(jnp.bfloat16)
    probe_lines = probe_row.shape[0]
    asked = jnp.concatenate([queries, probe_row], axis=0)
    lanes = 128
    asks, feats_all = exchange(
        [(asked.reshape(-1, lanes), "clus", True), (jnp.transpose(item_feats), "feat", True)],
        AXES,
        sizes,
        0,
    )
    asks = asks.reshape((owner_count,) + asked.shape)

    pre_act = jnp.einsum(
        "ski,skh->ih",
        feats_all,
        w_hidden.reshape(feat_count, -1, w_hidden.shape[1]),
        preferred_element_type=jnp.float32,
    )
    hidden = jax.nn.silu(pre_act + b_hidden.astype(jnp.float32)).astype(jnp.bfloat16)
    partial = jnp.dot(hidden, w_out, preferred_element_type=jnp.float32)
    (parts,) = exchange(
        [(partial.reshape(feat_count, device_rows, -1), "feat", False)], AXES, sizes, 1
    )
    projected = jnp.sum(parts, axis=0)
    scaling = lax.rsqrt(jnp.mean(projected * projected, axis=1, keepdims=True) + 1e-06) * unit_scale
    embedded = (projected * scaling).astype(jnp.bfloat16)

    my_clusters = lax.dynamic_slice_in_dim(item_cluster, feat_index * device_rows, device_rows, 0)
    all_queries = asks[:, :query_count].reshape(-1, emb_width)
    all_probes = (
        asks[:, query_count : query_count + probe_lines]
        .astype(jnp.int32)
        .reshape(owner_count, probe_count, query_count)
    )

    first_owned = owner_index * owned_count
    local_ids = jnp.arange(owned_count, dtype=jnp.int32)
    owned_ids = first_owned + local_ids
    row_number = feat_index * row_dev + jnp.arange(row_dev, dtype=jnp.int32)
    stored_live = row_number[None, :] < cluster_fill[:, None]
    slot_ids = jnp.arange(cluster_slot.shape[0], dtype=jnp.int32)
    owned_clusters = jnp.sum(
        jnp.where(cluster_slot[None, :] == owned_ids[:, None], slot_ids[None, :], 0), axis=1
    )
    probed = jnp.any(all_probes[..., None] == owned_clusters, axis=1).reshape(-1, owned_count)
    stored_allowed = (jnp.transpose(probed)[:, None, :] & stored_live[:, :, None]).reshape(
        owned_count * row_dev, -1
    )
    fresh_allowed = jnp.any(
        my_clusters[:, None, None, None] == all_probes[None], axis=2
    ).reshape(device_rows, -1)
    pad_rows = 2 * TOPK - owned_count * row_dev - device_rows
    allowed = jnp.concatenate(
        [stored_allowed, fresh_allowed, jnp.zeros((pad_rows, stored_allowed.shape[1]), bool)],
        axis=0,
    )
    scored_rows = jnp.concatenate(
        [
            catalog.reshape(owned_count * row_dev, emb_width),
            embedded,
            jnp.zeros((pad_rows, emb_width), embedded.dtype),
        ],
        0,
    )
    scores = jnp.einsum("rd,bd->rb", scored_rows, all_queries, preferred_element_type=jnp.float32)
    scores = jnp.where(allowed, scores, masked_score)
    local_best = top_half(scores)

    (arrived,) = exchange(
        [(local_best.reshape(owner_count, query_count, -1), "clus", False)], AXES, sizes, 3
    )
    sublanes, lanes = 8, 128
    groups = lanes // query_count
    steps = [(2, query_count * 2**i) for i in range(groups.bit_length() - 1)]
    steps += [(1, 2**i) for i in range(sublanes.bit_length() - 1)]
    narrowed = merge_lists(arrived.reshape(-1, arrived.shape[2]), tuple(steps), query_count)
    (gathered,) = exchange([(narrowed, "feat", True)], AXES, sizes, 4)
    steps = [(1, 2**i) for i in range(feat_count.bit_length() - 1)]
    return merge_lists(gathered.reshape(-1, gathered.shape[2]), tuple(steps), query_count)


def solution(mesh):
    return jax.shard_map(
        body,
        mesh=mesh,
        in_specs=(
            P("clus", "feat"),
            P(None, "feat"),
            P("feat"),
            P("feat", None),
            P("clus"),
            P(),
            P("clus", "feat", None),
            P("clus"),
            P("clus", None),
            P("clus", None),
        ),
        out_specs=P("clus", None),
        check_vma=False,
    )
```
